512 devices in a mesh: row: 16 (over x, z_lo), col: 32 (over y, z_hi, core).
Axes of the slice: x: 4, y: 8, z: 8 (z_hi: 2, z_lo: 4; z = z_hi * 4 + z_lo), core: 2. Of those that a mesh axis runs over, the one named last changes fastest.
Arguments:
- amplitudes: float32 [32, 96, 4, 128, 128], P('col', 'row'), may hold values from -6 to 6
- integrals: float32 [2, 2048, 16384], P(None, 'row', 'col'), may hold values from -0.25 to 0.25
- owner_column: int32 [2], replicated, may hold values from 0 to 31
- occ_irrep: int32 [96], replicated, may hold values from 0 to 7, as said below
- pair_irrep: int32 [2, 16], replicated, may hold values from 0 to 7, as said below
Outputs:
- ladder: float32 [12288, 16384], P('row', 'col')
The draws below stay inside these ranges and needn't reach their ends.
Inputs may be any that keep to these rules, and one draw needn't show every extreme that they name: `occ_irrep`: every irrep 0 to 7 labels some occupied-pair tile. `pair_irrep`: in each section no irrep labels more than 4 of the 16 panel tiles, and some irrep labels exactly 4.
All inputs are finite; a program needn't handle non-finite values.
Results may differ from the reference program's by a relative error of at most 0.0001.
Values sent between devices are 32-bit elements; how exact they have to be, the bound alone decides.
A program may use at most 64 MiB of HBM per device.

```python
import jax
import jax.numpy as jnp
from jax import lax

TILE = 128
IRREPS = 8
SECTIONS = 2
OCC_TILES = 96
KT = 16
CAP = 4
NVV = 16384
N_COL = 32


def draw_occ_irrep(key, part):
    label_key, place_key = jax.random.split(key)
    labels = jax.random.randint(label_key, (OCC_TILES,), 0, IRREPS, dtype=jnp.int32)
    places = jax.random.permutation(place_key, OCC_TILES)[:IRREPS]
    return labels.at[places].set(jnp.arange(IRREPS, dtype=jnp.int32))


def section_labels(key):
    busy_key, rotation_key, order_key = jax.random.split(key, 3)
    busiest = jax.random.randint(busy_key, (), 0, IRREPS, dtype=jnp.int32)
    free_turn = jax.random.randint(rotation_key, (), 0, IRREPS - 1, dtype=jnp.int32)
    rotation = jnp.where(busiest == IRREPS - 1, free_turn, IRREPS - 2 - busiest).astype(jnp.int32)
    remaining = (busiest + 1 + (jnp.arange(KT - CAP, dtype=jnp.int32) + rotation) % (IRREPS - 1)) % IRREPS
    listed = jnp.concatenate([jnp.full((CAP,), busiest, jnp.int32), remaining.astype(jnp.int32)])
    return listed[jax.random.permutation(order_key, KT)]


def draw_pair_irrep(key, part):
    return jax.vmap(section_labels)(jax.random.split(key, SECTIONS))


def shard_levels(key, shape, cuts, smallest, largest):
    level, own = 1.0, jax.random.fold_in(key, 6)
    for position, parts in cuts:
        steps = jnp.exp(jax.random.uniform(jax.random.fold_in(own, position), (parts,), jnp.float32, smallest / len(cuts), largest / len(cuts)))
        level = level * jnp.repeat(steps, shape[position] // parts).reshape([-1 if axis == position else 1 for axis in range(len(shape))])
    return level


def centred(key, shape, scale, bound, shards=(), kind=jnp.bfloat16):
    values = scale * jax.random.normal(key, shape, jnp.float32)
    if shards:
        values = values * shard_levels(key, shape, shards, -0.22, 0.18)
    return jnp.clip(values, -bound, bound).astype(kind)


def setup_inputs(seed: int = 0) -> dict:
    splits = jax.random.split(jax.random.key(seed), 6)
    amplitudes = centred(splits[0], (N_COL, OCC_TILES, CAP, TILE, TILE), 1.0, 6.0, ((0, 32), (1, 16)), jnp.float32)
    integrals = centred(splits[1], (SECTIONS, KT * TILE, NVV), (KT * TILE * SECTIONS // IRREPS) ** -0.5, 0.25, ((1, 16), (2, 32)), jnp.float32)
    owner_column = jax.random.randint(splits[2], (SECTIONS,), 0, N_COL).astype(jnp.int32)
    occ_irrep = draw_occ_irrep(jax.random.fold_in(splits[5], 71), 0)
    pair_irrep = draw_pair_irrep(jax.random.fold_in(splits[5], 71), 0)
    return dict(amplitudes=amplitudes, integrals=integrals, owner_column=owner_column, occ_irrep=occ_irrep, pair_irrep=pair_irrep)


def slot_tables(occ_labels, pair_labels):
    matches = occ_labels[:, None] == pair_labels[None, :]
    order_rank = jnp.cumsum(matches.astype(jnp.int32), axis=1) - 1
    slot_ids = jnp.arange(CAP, dtype=jnp.int32)
    chosen = matches[:, None, :] & (order_rank[:, None, :] == slot_ids[None, :, None])
    positions = jnp.arange(pair_labels.shape[0], dtype=jnp.int32)
    tile_index = jnp.sum(chosen.astype(jnp.int32) * positions[None, None, :], axis=2).astype(jnp.int32)
    valid_slot = jnp.any(chosen, axis=2)
    return tile_index, valid_slot


def reference(amplitudes, integrals, owner_column, occ_irrep, pair_irrep):
    ladder = jnp.zeros((OCC_TILES, TILE, NVV), jnp.float32)
    for which_section in range(SECTIONS):
        tile_index, valid_slot = slot_tables(occ_irrep, pair_irrep[which_section])
        amp_panel = amplitudes[owner_column[which_section]] * valid_slot[:, :, None, None].astype(jnp.float32)
        row_tiles = integrals[which_section].reshape(KT, TILE, NVV)

        def one_tile(operands):
            amp_tile, index_row = operands
            picked = jnp.take(row_tiles, index_row, axis=0)
            return jnp.einsum("sij,sjv->iv", amp_tile, picked, precision=lax.Precision.HIGHEST)

        ladder = ladder + lax.map(one_tile, (amp_panel, tile_index))
    return ladder.reshape(OCC_TILES * TILE, NVV)
```

```python
import functools

import jax
import jax.numpy as jnp
from jax import lax
from jax.experimental import pallas as pl
from jax.experimental.pallas import tpu as pltpu
from jax.sharding import PartitionSpec as P

MESH = pl.DeviceIdType.MESH
NX, NZ, NY, NH, NC = 4, 4, 8, 2, 2
TILE = 128
X_ROWS = 24
OFFSETS = (0, -1, 1, -2, 2, -3, 3)


class Copy:
    def __init__(self, src, dst, landing, send, recv, device, sends=None, receives=None):
        self.out = (src, dst, send, recv, device)
        self.into = (landing, landing, send, recv, device)
        self.sends, self.receives = sends, receives

    def start(self):
        guarded(self.sends, lambda: remote(*self.out).start())

    def wait_recv(self):
        guarded(self.receives, lambda: remote(*self.into).wait_recv())

    def wait_send(self):
        guarded(self.sends, lambda: remote(*self.out).wait_send())


def remote(src, dst, send, recv, device):
    return pltpu.make_async_remote_copy(
        src_ref=src, dst_ref=dst, send_sem=send, recv_sem=recv, device_id=device, device_id_type=MESH
    )


def guarded(condition, action):
    if condition is None:
        action()
    else:
        pl.when(condition)(action)


def multiply(occ_ref, pair_ref, first, panel, held, out_ref):
    sections, positions = pair_ref.shape
    slots = panel.shape[1] // (TILE * out_ref.shape[0] // TILE)
    bf, f32 = jnp.bfloat16, jnp.float32

    def split(value):
        high = value.astype(bf)
        return high, (value - high.astype(f32)).astype(bf)

    def one(o, carry):
        label = occ_ref[first + o]
        total = jnp.zeros((TILE, out_ref.shape[1]), f32)
        for k in range(sections):
            count = jnp.int32(0)
            index = [jnp.int32(0)] * slots
            for t in range(positions):
                match = pair_ref[k, t] == label
                for s in range(min(slots, t + 1)):
                    index[s] = jnp.where(match & (count == s), t, index[s])
                count = count + match.astype(jnp.int32)
            for pair in range(slots // 2):
                left, right = [], []
                for s in (2 * pair, 2 * pair + 1):
                    rows = pl.multiple_of((o * slots + s) * TILE, TILE)
                    tile = panel[k, pl.ds(rows, TILE), :]
                    left.append(jnp.where(count > s, tile, 0.0))
                    right.append(held[k, index[s] // NZ, index[s] % NZ])
                a_high, a_low = split(jnp.concatenate(left, axis=1))
                b_high, b_low = split(jnp.concatenate(right, axis=0))
                dot = functools.partial(jnp.dot, preferred_element_type=f32)
                total = total + (dot(a_high, b_high) + (dot(a_high, b_low) + dot(a_low, b_high)))
        out_ref[pl.ds(pl.multiple_of(o * TILE, TILE), TILE), :] = total
        return carry

    lax.fori_loop(0, out_ref.shape[0] // TILE, one, 0)


def kernel(owner_ref, occ_ref, pair_ref, amp_ref, int_ref, out_ref, held, panel, both, right_out, right_in,
           left_out, left_in, mine_out, other_in, local_sem, z_sem, x_sem, xf_sem, xz_sem, rs_sem, ag_sem, sib_sem,
           cross_sem):
    row, col = lax.axis_index("row"), lax.axis_index("col")
    x, z = row // NZ, row % NZ
    y, h, c = col // (NH * NC), (col // NC) % NH, col % NC

    def device(dx=0, dz=0, dy=0, flip_h=False, flip_c=False):
        h2 = 1 - h if flip_h else h
        c2 = 1 - c if flip_c else c
        return (((x + dx + NX) % NX) * NZ + z + dz, ((y + dy + NY) % NY) * (NH * NC) + h2 * NC + c2)

    sections = int_ref.shape[0]
    half = amp_ref.shape[0] // NC
    share = half // NY
    events = []

    def at(time, action):
        events.append((time, len(events), action))

    sent = []

    def go(copy):
        copy.start()
        sent.append(copy)

    barrier = pltpu.get_barrier_semaphore()
    partners = [device(dx=1), device(dx=-1), device(dy=1), device(dy=-1), device(flip_h=True), device(flip_c=True)]
    for partner in partners:
        pl.semaphore_signal(barrier, inc=1, device_id=partner, device_id_type=MESH)

    @pl.when(z > 0)
    def _():
        pl.semaphore_signal(barrier, inc=1, device_id=device(dz=-1), device_id_type=MESH)

    @pl.when(z < NZ - 1)
    def _():
        pl.semaphore_signal(barrier, inc=1, device_id=device(dz=1), device_id_type=MESH)

    own_ints = pltpu.make_async_copy(int_ref, held.at[:, x, z], local_sem.at[0])
    own_half = pltpu.make_async_copy(
        amp_ref.at[pl.ds(pl.multiple_of(c * half, 8), half), :], both.at[c], local_sem.at[1])
    own_ints.start()
    own_half.start()
    pl.semaphore_wait(barrier, len(partners) + (z > 0).astype(jnp.int32) + (z < NZ - 1).astype(jnp.int32))

    unit = 5.2 * (TILE - X_ROWS) / TILE

    zr = pl.ds(X_ROWS, TILE - X_ROWS)
    mid = (TILE - X_ROWS) // 16 * 8
    low, high = pl.ds(X_ROWS, mid), pl.ds(X_ROWS + mid, TILE - X_ROWS - mid)

    def z_copy(k, s, way):
        src = int_ref.at[k, zr] if s == 1 else held.at[k, x, z - way * (s - 1), zr]
        to = held.at[k, x, z - way * (s - 1), zr]
        frm = held.at[k, x, z - way * s, zr]
        if way > 0:
            sends, receives = (z < NZ - 1) & (z - (s - 1) >= 0), z - s >= 0
        else:
            sends, receives = (z > 0) & (z + (s - 1) <= NZ - 1), z + s <= NZ - 1
        w = 0 if way > 0 else 1
        return Copy(src, to, frm, z_sem.at[0, k, s - 1, w], z_sem.at[1, k, s - 1, w], device(dz=way), sends, receives)

    def x_copy(k, d, way):
        zz = z + d
        valid = None if d == 0 else (zz >= 0) & (zz <= NZ - 1)
        src = int_ref.at[k, zr] if d == 0 else held.at[k, x, zz, zr]
        w = 0 if way > 0 else 1
        return Copy(src, held.at[k, x, zz, zr], held.at[k, (x - way + NX) % NX, zz, zr],
                    x_sem.at[0, k, zz, w], x_sem.at[1, k, zz, w], device(dx=way), valid, valid)

    def x_forward(k, d, way):
        zz = z + d
        valid = None if d == 0 else (zz >= 0) & (zz <= NZ - 1)
        rows = low if way > 0 else high
        xs = (x - way + NX) % NX
        w = 2 if way > 0 else 3
        return Copy(held.at[k, xs, zz, rows], held.at[k, xs, zz, rows], held.at[k, (x + 2) % NX, zz, rows],
                    x_sem.at[0, k, zz, w], x_sem.at[1, k, zz, w], device(dx=way), valid, valid)

    def step_time(k, d):
        return 1.5 * unit * (2 * abs(d) + k)

    for k in range(sections):
        for way in (1, -1):
            at(0.01 + 0.1 * k, lambda k=k, way=way: go(z_copy(k, 1, way)))
            at(0.02 + 0.1 * k, lambda k=k, way=way: go(x_copy(k, 0, way)))
        for d in OFFSETS:
            if d:
                way, s = (1, -d) if d < 0 else (-1, d)

                def arrived(k=k, d=d, way=way, s=s):
                    z_copy(k, s, way).wait_recv()
                    if s < NZ - 1:
                        go(z_copy(k, s + 1, way))
                    for side in (1, -1):
                        go(x_copy(k, d, side))

                at((unit + 3.9 * X_ROWS / 24) * (s - 1) + unit * (k + 1), arrived)

            def passed(k=k, d=d):
                for side in (1, -1):
                    x_copy(k, d, side).wait_recv()
                    go(x_forward(k, d, side))

            def ended(k=k, d=d):
                for side in (1, -1):
                    x_forward(k, d, side).wait_recv()

            begin = max(step_time(k, d), (unit + 3.9 * X_ROWS / 24) * (abs(d) - 1) + unit * (k + 1) + 0.02 if d else 0.3)
            at(begin + unit, passed)
            at(begin + 1.8 * unit + 3, ended)

    if X_ROWS:
        xr = pl.ds(0, X_ROWS)
        cut = X_ROWS // 16 * 8
        xlow, xhigh = pl.ds(0, cut), pl.ds(cut, X_ROWS - cut)

        def f_copy(k, way):
            w = 0 if way > 0 else 1
            return Copy(int_ref.at[k, xr], held.at[k, x, z, xr], held.at[k, (x - way + NX) % NX, z, xr],
                        xf_sem.at[0, k, w], xf_sem.at[1, k, w], device(dx=way))

        def f_forward(k, way):
            rows = xlow if way > 0 else xhigh
            xs = (x - way + NX) % NX
            w = 2 if way > 0 else 3
            return Copy(held.at[k, xs, z, rows], held.at[k, xs, z, rows], held.at[k, (x + 2) % NX, z, rows],
                        xf_sem.at[0, k, w], xf_sem.at[1, k, w], device(dx=way))

        def fz_copy(k, s, way):
            to = held.at[k, :, z - way * (s - 1), xr]
            frm = held.at[k, :, z - way * s, xr]
            if way > 0:
                sends, receives = (z < NZ - 1) & (z - (s - 1) >= 0), z - s >= 0
            else:
                sends, receives = (z > 0) & (z + (s - 1) <= NZ - 1), z + s <= NZ - 1
            w = 0 if way > 0 else 1
            return Copy(to, to, frm, xz_sem.at[0, k, s - 1, w], xz_sem.at[1, k, s - 1, w], device(dz=way), sends, receives)

        for k in range(sections):
            for way in (1, -1):
                at(0.0 + 0.1 * k, lambda k=k, way=way: go(f_copy(k, way)))

            def near(k=k):
                for way in (1, -1):
                    f_copy(k, way).wait_recv()
                    go(f_forward(k, way))

            def far(k=k):
                for way in (1, -1):
                    f_forward(k, way).wait_recv()
                if k == 0:
                    own_ints.wait()
                for way in (1, -1):
                    go(fz_copy(k, 1, way))

            at(2.0 + k * 0.2, near)
            at(4.0 + k * 0.2, far)
            for s in range(1, NZ):

                def climb(k=k, s=s):
                    for way in (1, -1):
                        fz_copy(k, s, way).wait_recv()
                        if s < NZ - 1:
                            go(fz_copy(k, s + 1, way))

                at((2 * unit + 7.8 * X_ROWS / 24) * s + 2.0 * k, climb)
    else:
        at(4.0, own_ints.wait)

    def half_rows(core):
        return pl.ds(pl.multiple_of(core * half, 8), half)

    swap = Copy(amp_ref.at[half_rows(1 - c), :], both.at[c], both.at[1 - c], sib_sem.at[0, sections, 0],
                sib_sem.at[1, sections, 0], device(flip_c=True))

    owner_y = [owner_ref[k] // (NH * NC) for k in range(sections)]
    owner_h = [(owner_ref[k] // NC) % NH for k in range(sections)]
    owner_c = [owner_ref[k] % NC for k in range(sections)]

    def stored(k, j):
        rows = pl.ds(pl.multiple_of(j * share, 8), share)
        return jnp.where(owner_c[k] == 0, both[0, rows, :], both[1, rows, :])

    def rs_copy(k, i, way):
        w = 0 if way > 0 else 1
        src, dst = (right_out, right_in) if way > 0 else (left_out, left_in)
        return Copy(src.at[k, i], dst.at[k, i], dst.at[k, i], rs_sem.at[0, k, i, w], rs_sem.at[1, k, i, w], device(dy=way))

    def rs_send(k, i, way):
        j = (y + 4 - i) % NY if way > 0 else (y - 3 + i + NY) % NY
        src, dst = (right_out, right_in) if way > 0 else (left_out, left_in)
        value = stored(k, j)
        if i:
            value = jnp.where(owner_y[k] == y, value, dst[k, i - 1])
        src[k, i] = value
        go(rs_copy(k, i, way))

    def cross_copy(k):
        return Copy(mine_out.at[k], other_in.at[k], other_in.at[k], cross_sem.at[0, k], cross_sem.at[1, k],
                    device(flip_h=True))

    def share_rows(j, core):
        return pl.ds(pl.multiple_of(core * half + j * share, 8), share)

    def ag_copy(k, i, way):
        j = (y - way * i + NY) % NY
        g = (y - way * (i + 1) + NY) % NY
        w = 0 if way > 0 else 1
        return Copy(panel.at[k, share_rows(j, c), :], panel.at[k, share_rows(j, c), :], panel.at[k, share_rows(g, c), :],
                    ag_sem.at[0, k, i, w], ag_sem.at[1, k, i, w], device(dy=way))

    def sib_copy(k, d):
        j = (y - d + NY) % NY
        n = d + 3
        return Copy(panel.at[k, share_rows(j, c), :], panel.at[k, share_rows(j, c), :], panel.at[k, share_rows(j, 1 - c), :],
                    sib_sem.at[0, k, n], sib_sem.at[1, k, n], device(flip_c=True))

    def begin_rs():
        own_half.wait()
        swap.wait_recv()

    at(-0.5, lambda: go(swap))
    at(2.9, begin_rs)
    for k in range(sections):
        def first(k=k):
            for way in (1, -1):
                rs_send(k, 0, way)

        at(3.0 + 0.1 * k, first)
        for i in range(4):
            def advance(k=k, i=i):
                for way in (1, -1):
                    if way > 0 or i < 3:
                        rs_copy(k, i, way).wait_recv()
                    if i < (3 if way > 0 else 2):
                        rs_send(k, i + 1, way)
                if i == 3:
                    ahead = (owner_y[k] - y + NY) % NY
                    value = jnp.where(ahead == 0, stored(k, y), jnp.where(ahead <= 3, left_in[k, 2], right_in[k, 3]))
                    mine_out[k] = value
                    go(cross_copy(k))

            at(4.0 + 4.5 * (i + 1) + 2.0 * k, advance)

        def crossed(k=k):
            cross_copy(k).wait_recv()
            panel[k, share_rows(y, c), :] = jnp.where(owner_h[k] == h, mine_out[k], other_in[k])
            for way in (1, -1):
                go(ag_copy(k, 0, way))
            go(sib_copy(k, 0))

        at(28.0 + 2.0 * k, crossed)
        for i in range(4):
            def gathered(k=k, i=i):
                for way in (1, -1):
                    if way < 0 and i == 3:
                        continue
                    ag_copy(k, i, way).wait_recv()
                    if i < (3 if way > 0 else 2):
                        go(ag_copy(k, i + 1, way))
                    go(sib_copy(k, way * (i + 1)))

            at(28.0 + 4.5 * (i + 1) + 2.0 * k, gathered)

        def complete(k=k):
            for d in range(-3, 5):
                sib_copy(k, d).wait_recv()

        at(50.0 + k, complete)

    for _, _, action in sorted(events, key=lambda event: event[:2]):
        action()
    multiply(occ_ref, pair_ref, row * (out_ref.shape[0] // TILE), panel, held, out_ref)
    for copy in sent:
        copy.wait_send()


def on_device(amplitudes, integrals, owner_column, occ_irrep, pair_irrep):
    tiles_here, slots, tile = amplitudes.shape[1:4]
    sections, _, columns = integrals.shape
    rows = tiles_here * slots * tile
    half, share = rows // NC, rows // NC // NY
    f32 = jnp.float32
    dma = pltpu.SemaphoreType.DMA
    smem = pl.BlockSpec(memory_space=pltpu.SMEM)
    return pl.pallas_call(
        kernel,
        out_shape=jax.ShapeDtypeStruct((tiles_here * tile, columns), f32),
        in_specs=[smem, smem, smem, pl.BlockSpec(memory_space=pl.ANY), pl.BlockSpec(memory_space=pl.ANY)],
        out_specs=pl.BlockSpec(memory_space=pltpu.VMEM),
        scratch_shapes=[
            pltpu.VMEM((sections, NX, NZ, tile, columns), f32),
            pltpu.VMEM((sections, rows, tile), f32),
            pltpu.VMEM((NC, half, tile), f32),
            pltpu.VMEM((sections, 4, share, tile), f32),
            pltpu.VMEM((sections, 4, share, tile), f32),
            pltpu.VMEM((sections, 3, share, tile), f32),
            pltpu.VMEM((sections, 3, share, tile), f32),
            pltpu.VMEM((sections, share, tile), f32),
            pltpu.VMEM((sections, share, tile), f32),
            dma((2,)),
            dma((2, sections, 3, 2)),
            dma((2, sections, 4, 4)),
            dma((2, sections, 4)),
            dma((2, sections, 3, 2)),
            dma((2, sections, 4, 2)),
            dma((2, sections, 4, 2)),
            dma((2, sections + 1, 8)),
            dma((2, sections)),
        ],
        compiler_params=pltpu.CompilerParams(
            collective_id=0, has_side_effects=True, vmem_limit_bytes=48 * 1024 * 1024
        ),
        name="ladder",
    )(owner_column, occ_irrep, pair_irrep, amplitudes.reshape(rows, tile), integrals)


def solution(mesh):
    return jax.shard_map(
        on_device,
        mesh=mesh,
        in_specs=(P("col", "row", None, None, None), P(None, "row", "col"), P(), P(), P()),
        out_specs=P("row", "col"),
        check_vma=False,
    )
```

```python
import functools

import jax
import jax.numpy as jnp
from jax import lax
from jax.experimental import pallas as pl
from jax.experimental.pallas import tpu as pltpu
from jax.sharding import PartitionSpec as P

MESH = pl.DeviceIdType.MESH
NX, NZ, NY, NH, NC = 4, 4, 8, 2, 2
TILE = 128
X_ROWS = 24
OFFSETS = (0, -1, 1, -2, 2, -3, 3)
ORDER = (
    ('swap',), ('z', 0, 1, -1), ('rs', 0, 0, 1), ('z', 0, 1, 1), ('rs', 0, 0, -1), ('z', 1, 1, -1),
    ('rs', 0, 1, -1), ('rs', 1, 0, 1), ('rs', 1, 0, -1), ('f', 0, 1), ('x', 0, 0, -1), ('f', 0, -1), ('z', 1, 1, 1),
    ('rs', 0, 1, 1), ('z', 0, 2, 1), ('f', 1, 1), ('rs', 1, 1, 1), ('z', 0, 2, -1), ('rs', 0, 2, 1),
    ('rs', 1, 2, 1), ('rs', 1, 1, -1), ('rs', 0, 2, -1), ('f', 1, -1), ('rs', 0, 3, 1), ('z', 0, 3, -1),
    ('rs', 1, 2, -1), ('x', 0, 0, 1), ('x', 1, 0, 1), ('rs', 1, 3, 1), ('x', 0, -1, -1), ('x', 0, 3, 1), ('fz', 0),
    ('x', 1, 1, 1), ('cross', 0), ('z', 1, 2, -1), ('ag', 0, 0, 1), ('x', 1, 0, -1), ('z', 1, 2, 1), ('x', 0, 2, 1),
    ('x', 0, -2, -1), ('x', 0, 2, -1), ('fz', 1), ('cross', 1), ('ag', 0, 1, 1), ('x', 0, -1, 1), ('z', 1, 3, 1),
    ('x', 0, 1, -1), ('ag', 1, 0, -1), ('ag', 0, 0, -1), ('x', 0, 1, 1), ('c', 0, 1, -1), ('ag', 1, 0, 1),
    ('z', 0, 3, 1), ('c', 0, 1, 1), ('c', 1, 1, -1), ('x', 1, -2, -1), ('ag', 1, 1, 1), ('x', 1, -2, 1),
    ('ag', 0, 2, 1), ('c', 1, 1, 1), ('x', 1, 2, 1), ('ag', 0, 1, -1), ('ag', 1, 1, -1), ('x', 0, -2, 1),
    ('x', 1, -3, -1), ('x', 1, 2, -1), ('x', 1, -1, -1), ('z', 1, 3, -1), ('ag', 0, 2, -1), ('x', 1, -1, 1),
    ('ag', 1, 2, 1), ('x', 0, 3, -1), ('x', 1, 3, 1), ('x', 1, 1, -1), ('ag', 0, 3, 1), ('c', 1, 2, -1),
    ('c', 0, 2, 1), ('ag', 1, 3, 1), ('x', 1, -3, 1), ('c', 0, 2, -1), ('ag', 1, 2, -1), ('x', 0, -3, 1),
    ('x', 1, 3, -1), ('x', 0, -3, -1), ('c', 1, 2, 1),
)


class Copy:
    def __init__(self, src, dst, landing, send, recv, device, sends=None, receives=None):
        self.out = (src, dst, send, recv, device)
        self.into = (landing, landing, send, recv, device)
        self.sends, self.receives = sends, receives

    def start(self):
        guarded(self.sends, lambda: remote(*self.out).start())

    def wait_recv(self):
        guarded(self.receives, lambda: remote(*self.into).wait_recv())

    def wait_send(self):
        guarded(self.sends, lambda: remote(*self.out).wait_send())


def remote(src, dst, send, recv, device):
    return pltpu.make_async_remote_copy(
        src_ref=src, dst_ref=dst, send_sem=send, recv_sem=recv, device_id=device, device_id_type=MESH
    )


def guarded(condition, action):
    if condition is None:
        action()
    else:
        pl.when(condition)(action)


def multiply(occ_ref, pair_ref, first, panel, held, out_ref):
    sections, positions = pair_ref.shape
    slots = panel.shape[1] // (TILE * out_ref.shape[0] // TILE)
    bf, f32 = jnp.bfloat16, jnp.float32

    def split(value):
        high = value.astype(bf)
        return high, (value - high.astype(f32)).astype(bf)

    def one(o, carry):
        label = occ_ref[first + o]
        total = jnp.zeros((TILE, out_ref.shape[1]), f32)
        for k in range(sections):
            count = jnp.int32(0)
            index = [jnp.int32(0)] * slots
            for t in range(positions):
                match = pair_ref[k, t] == label
                for s in range(min(slots, t + 1)):
                    index[s] = jnp.where(match & (count == s), t, index[s])
                count = count + match.astype(jnp.int32)
            for pair in range(slots // 2):
                left, right = [], []
                for s in (2 * pair, 2 * pair + 1):
                    rows = pl.multiple_of((o * slots + s) * TILE, TILE)
                    tile = panel[k, pl.ds(rows, TILE), :]
                    left.append(jnp.where(count > s, tile, 0.0))
                    right.append(held[k, index[s] // NZ, index[s] % NZ])
                a_high, a_low = split(jnp.concatenate(left, axis=1))
                b_high, b_low = split(jnp.concatenate(right, axis=0))
                dot = functools.partial(jnp.dot, preferred_element_type=f32)
                total = total + (dot(a_high, b_high) + (dot(a_high, b_low) + dot(a_low, b_high)))
        out_ref[pl.ds(pl.multiple_of(o * TILE, TILE), TILE), :] = total
        return carry

    lax.fori_loop(0, out_ref.shape[0] // TILE, one, 0)


def kernel(owner_ref, occ_ref, pair_ref, amp_ref, int_ref, out_ref, held, panel, both, right_out, right_in,
           left_out, left_in, mine_out, other_in, local_sem, z_sem, x_sem, xf_sem, xz_sem, rs_sem, ag_sem, sib_sem,
           cross_sem):
    row, col = lax.axis_index("row"), lax.axis_index("col")
    x, z = row // NZ, row % NZ
    y, h, c = col // (NH * NC), (col // NC) % NH, col % NC

    def device(dx=0, dz=0, dy=0, flip_h=False, flip_c=False):
        h2 = 1 - h if flip_h else h
        c2 = 1 - c if flip_c else c
        return (((x + dx + NX) % NX) * NZ + z + dz, ((y + dy + NY) % NY) * (NH * NC) + h2 * NC + c2)

    sections = int_ref.shape[0]
    half = amp_ref.shape[0] // NC
    share = half // NY
    events, last, sent = {}, [], []

    def go(copy):
        copy.start()
        sent.append(copy)

    barrier = pltpu.get_barrier_semaphore()
    partners = [device(dx=1), device(dx=-1), device(dy=1), device(dy=-1), device(flip_h=True), device(flip_c=True)]
    for partner in partners:
        pl.semaphore_signal(barrier, inc=1, device_id=partner, device_id_type=MESH)

    @pl.when(z > 0)
    def _():
        pl.semaphore_signal(barrier, inc=1, device_id=device(dz=-1), device_id_type=MESH)

    @pl.when(z < NZ - 1)
    def _():
        pl.semaphore_signal(barrier, inc=1, device_id=device(dz=1), device_id_type=MESH)

    own_ints = pltpu.make_async_copy(int_ref, held.at[:, x, z], local_sem.at[0])
    own_half = pltpu.make_async_copy(
        amp_ref.at[pl.ds(pl.multiple_of(c * half, 8), half), :], both.at[c], local_sem.at[1])
    own_ints.start()
    own_half.start()
    pl.semaphore_wait(barrier, len(partners) + (z > 0).astype(jnp.int32) + (z < NZ - 1).astype(jnp.int32))

    zr = pl.ds(X_ROWS, TILE - X_ROWS)
    mid = (TILE - X_ROWS) // 16 * 8
    low, high = pl.ds(X_ROWS, mid), pl.ds(X_ROWS + mid, TILE - X_ROWS - mid)

    def z_copy(k, s, way):
        src = int_ref.at[k, zr] if s == 1 else held.at[k, x, z - way * (s - 1), zr]
        to = held.at[k, x, z - way * (s - 1), zr]
        frm = held.at[k, x, z - way * s, zr]
        if way > 0:
            sends, receives = (z < NZ - 1) & (z - (s - 1) >= 0), z - s >= 0
        else:
            sends, receives = (z > 0) & (z + (s - 1) <= NZ - 1), z + s <= NZ - 1
        w = 0 if way > 0 else 1
        return Copy(src, to, frm, z_sem.at[0, k, s - 1, w], z_sem.at[1, k, s - 1, w], device(dz=way), sends, receives)

    def x_copy(k, d, way):
        zz = z + d
        valid = None if d == 0 else (zz >= 0) & (zz <= NZ - 1)
        src = int_ref.at[k, zr] if d == 0 else held.at[k, x, zz, zr]
        w = 0 if way > 0 else 1
        return Copy(src, held.at[k, x, zz, zr], held.at[k, (x - way + NX) % NX, zz, zr],
                    x_sem.at[0, k, zz, w], x_sem.at[1, k, zz, w], device(dx=way), valid, valid)

    def x_forward(k, d, way):
        zz = z + d
        valid = None if d == 0 else (zz >= 0) & (zz <= NZ - 1)
        rows = low if way > 0 else high
        xs = (x - way + NX) % NX
        w = 2 if way > 0 else 3
        return Copy(held.at[k, xs, zz, rows], held.at[k, xs, zz, rows], held.at[k, (x + 2) % NX, zz, rows],
                    x_sem.at[0, k, zz, w], x_sem.at[1, k, zz, w], device(dx=way), valid, valid)

    for k in range(sections):
        for d in OFFSETS:
            if d:
                way, s = (1, -d) if d < 0 else (-1, d)

                def arrived(k=k, d=d, way=way, s=s):
                    z_copy(k, s, way).wait_recv()
                    if s < NZ - 1:
                        go(z_copy(k, s + 1, way))
                    for side in (1, -1):
                        go(x_copy(k, d, side))

                events["z", k, s, way] = arrived
            for way in (1, -1):

                def passed(k=k, d=d, way=way):
                    x_copy(k, d, way).wait_recv()
                    go(x_forward(k, d, way))

                events["x", k, d, way] = passed
                last.append(x_forward(k, d, way))

    if X_ROWS:
        xr = pl.ds(0, X_ROWS)
        cut = X_ROWS // 16 * 8
        xlow, xhigh = pl.ds(0, cut), pl.ds(cut, X_ROWS - cut)

        def f_copy(k, way):
            w = 0 if way > 0 else 1
            return Copy(int_ref.at[k, xr], held.at[k, x, z, xr], held.at[k, (x - way + NX) % NX, z, xr],
                        xf_sem.at[0, k, w], xf_sem.at[1, k, w], device(dx=way))

        def f_forward(k, way):
            rows = xlow if way > 0 else xhigh
            xs = (x - way + NX) % NX
            w = 2 if way > 0 else 3
            return Copy(held.at[k, xs, z, rows], held.at[k, xs, z, rows], held.at[k, (x + 2) % NX, z, rows],
                        xf_sem.at[0, k, w], xf_sem.at[1, k, w], device(dx=way))

        def fz_copy(k, s, way):
            to = held.at[k, :, z - way * (s - 1), xr]
            frm = held.at[k, :, z - way * s, xr]
            if way > 0:
                sends, receives = (z < NZ - 1) & (z - (s - 1) >= 0), z - s >= 0
            else:
                sends, receives = (z > 0) & (z + (s - 1) <= NZ - 1), z + s <= NZ - 1
            w = 0 if way > 0 else 1
            return Copy(to, to, frm, xz_sem.at[0, k, s - 1, w], xz_sem.at[1, k, s - 1, w], device(dz=way), sends, receives)

        for k in range(sections):
            for way in (1, -1):

                def near(k=k, way=way):
                    f_copy(k, way).wait_recv()
                    go(f_forward(k, way))

                events["f", k, way] = near
                for s in range(1, NZ - 1):

                    def climb(k=k, s=s, way=way):
                        fz_copy(k, s, way).wait_recv()
                        go(fz_copy(k, s + 1, way))

                    events["c", k, s, way] = climb
                last.append(fz_copy(k, NZ - 1, way))

            def far(k=k):
                for way in (1, -1):
                    f_forward(k, way).wait_recv()
                for way in (1, -1):
                    go(fz_copy(k, 1, way))

            events["fz", k] = far

    def half_rows(core):
        return pl.ds(pl.multiple_of(core * half, 8), half)

    swap = Copy(amp_ref.at[half_rows(1 - c), :], both.at[c], both.at[1 - c], sib_sem.at[0, sections, 0],
                sib_sem.at[1, sections, 0], device(flip_c=True))

    owner_y = [owner_ref[k] // (NH * NC) for k in range(sections)]
    owner_h = [(owner_ref[k] // NC) % NH for k in range(sections)]
    owner_c = [owner_ref[k] % NC for k in range(sections)]

    def stored(k, j):
        rows = pl.ds(pl.multiple_of(j * share, 8), share)
        return jnp.where(owner_c[k] == 0, both[0, rows, :], both[1, rows, :])

    def rs_copy(k, i, way):
        w = 0 if way > 0 else 1
        src, dst = (right_out, right_in) if way > 0 else (left_out, left_in)
        return Copy(src.at[k, i], dst.at[k, i], dst.at[k, i], rs_sem.at[0, k, i, w], rs_sem.at[1, k, i, w], device(dy=way))

    def rs_send(k, i, way):
        j = (y + 4 - i) % NY if way > 0 else (y - 3 + i + NY) % NY
        src, dst = (right_out, right_in) if way > 0 else (left_out, left_in)
        value = stored(k, j)
        if i:
            value = jnp.where(owner_y[k] == y, value, dst[k, i - 1])
        src[k, i] = value
        go(rs_copy(k, i, way))

    def cross_copy(k):
        return Copy(mine_out.at[k], other_in.at[k], other_in.at[k], cross_sem.at[0, k], cross_sem.at[1, k],
                    device(flip_h=True))

    def share_rows(j, core):
        return pl.ds(pl.multiple_of(core * half + j * share, 8), share)

    def ag_copy(k, i, way):
        j = (y - way * i + NY) % NY
        g = (y - way * (i + 1) + NY) % NY
        w = 0 if way > 0 else 1
        return Copy(panel.at[k, share_rows(j, c), :], panel.at[k, share_rows(j, c), :], panel.at[k, share_rows(g, c), :],
                    ag_sem.at[0, k, i, w], ag_sem.at[1, k, i, w], device(dy=way))

    def sib_copy(k, d):
        j = (y - d + NY) % NY
        n = d + 3
        return Copy(panel.at[k, share_rows(j, c), :], panel.at[k, share_rows(j, c), :], panel.at[k, share_rows(j, 1 - c), :],
                    sib_sem.at[0, k, n], sib_sem.at[1, k, n], device(flip_c=True))

    def swapped():
        own_half.wait()
        swap.wait_recv()
        for k in range(sections):
            for way in (1, -1):
                rs_send(k, 0, way)

    events["swap",] = swapped
    steps = {1: NY // 2, -1: NY // 2 - 1}
    for k in range(sections):
        ended = []
        for way in (1, -1):
            for i in range(steps[way]):

                def advance(k=k, i=i, way=way, ended=ended):
                    rs_copy(k, i, way).wait_recv()
                    if i < steps[way] - 1:
                        rs_send(k, i + 1, way)
                    else:
                        ended.append(way)
                    if len(ended) == 2:
                        ended.append(0)
                        ahead = (owner_y[k] - y + NY) % NY
                        mine_out[k] = jnp.where(
                            ahead == 0, stored(k, y), jnp.where(ahead <= 3, left_in[k, 2], right_in[k, 3]))
                        go(cross_copy(k))

                def gathered(k=k, i=i, way=way):
                    ag_copy(k, i, way).wait_recv()
                    if i < steps[way] - 1:
                        go(ag_copy(k, i + 1, way))
                    go(sib_copy(k, way * (i + 1)))

                events["rs", k, i, way] = advance
                events["ag", k, i, way] = gathered

        def crossed(k=k):
            cross_copy(k).wait_recv()
            panel[k, share_rows(y, c), :] = jnp.where(owner_h[k] == h, mine_out[k], other_in[k])
            for way in (1, -1):
                go(ag_copy(k, 0, way))
            go(sib_copy(k, 0))

        events["cross", k] = crossed
        last.extend(sib_copy(k, d) for d in range(-3, 5))

    go(swap)
    for k in range(sections):
        for way in (1, -1):
            go(z_copy(k, 1, way))
        for way in (1, -1):
            go(x_copy(k, 0, way))
    if X_ROWS:
        for k in range(sections):
            for way in (1, -1):
                go(f_copy(k, way))
        own_ints.wait()
    for key in ORDER:
        events.pop(key)()
    if not X_ROWS:
        own_ints.wait()
    assert not events
    for copy in last:
        copy.wait_recv()
    multiply(occ_ref, pair_ref, row * (out_ref.shape[0] // TILE), panel, held, out_ref)
    for copy in sent:
        copy.wait_send()


def on_device(amplitudes, integrals, owner_column, occ_irrep, pair_irrep):
    tiles_here, slots, tile = amplitudes.shape[1:4]
    sections, _, columns = integrals.shape
    rows = tiles_here * slots * tile
    half, share = rows // NC, rows // NC // NY
    f32 = jnp.float32
    dma = pltpu.SemaphoreType.DMA
    smem = pl.BlockSpec(memory_space=pltpu.SMEM)
    return pl.pallas_call(
        kernel,
        out_shape=jax.ShapeDtypeStruct((tiles_here * tile, columns), f32),
        in_specs=[smem, smem, smem, pl.BlockSpec(memory_space=pl.ANY), pl.BlockSpec(memory_space=pl.ANY)],
        out_specs=pl.BlockSpec(memory_space=pltpu.VMEM),
        scratch_shapes=[
            pltpu.VMEM((sections, NX, NZ, tile, columns), f32),
            pltpu.VMEM((sections, rows, tile), f32),
            pltpu.VMEM((NC, half, tile), f32),
            pltpu.VMEM((sections, 4, share, tile), f32),
            pltpu.VMEM((sections, 4, share, tile), f32),
            pltpu.VMEM((sections, 3, share, tile), f32),
            pltpu.VMEM((sections, 3, share, tile), f32),
            pltpu.VMEM((sections, share, tile), f32),
            pltpu.VMEM((sections, share, tile), f32),
            dma((2,)),
            dma((2, sections, 3, 2)),
            dma((2, sections, 4, 4)),
            dma((2, sections, 4)),
            dma((2, sections, 3, 2)),
            dma((2, sections, 4, 2)),
            dma((2, sections, 4, 2)),
            dma((2, sections + 1, 8)),
            dma((2, sections)),
        ],
        compiler_params=pltpu.CompilerParams(
            collective_id=0, has_side_effects=True, vmem_limit_bytes=60 * 1024 * 1024
        ),
        name="ladder",
    )(owner_column, occ_irrep, pair_irrep, amplitudes.reshape(rows, tile), integrals)


def solution(mesh):
    return jax.shard_map(
        on_device,
        mesh=mesh,
        in_specs=(P("col", "row", None, None, None), P(None, "row", "col"), P(), P(), P()),
        out_specs=P("row", "col"),
        check_vma=False,
    )
```

```python
import functools

import jax
import jax.numpy as jnp
from jax import lax
from jax.experimental import pallas as pl
from jax.experimental.pallas import tpu as pltpu
from jax.sharding import PartitionSpec as P

MESH = pl.DeviceIdType.MESH
NX, NZ, NY, NH, NC = 4, 4, 8, 2, 2
TILE = 128
X_ROWS = (24, 16)
OFFSETS = (0, -1, 1, -2, 2, -3, 3)
ORDER = (
    ('fs', 1), ('swap',), ('z', 0, 1, -1), ('fs', 0), ('rs', 0, 0, 1), ('z', 0, 1, 1), ('z', 1, 1, 1),
    ('rs', 1, 0, 1), ('z', 1, 1, -1), ('rs', 0, 0, -1), ('rs', 1, 0, -1), ('rs', 0, 1, 1), ('rs', 1, 1, 1),
    ('z', 0, 2, 1), ('f', 0, -1), ('rs', 0, 1, -1), ('rs', 0, 2, 1), ('z', 0, 2, -1), ('rs', 1, 2, 1), ('f', 0, 1),
    ('f', 1, -1), ('f', 1, 1), ('rs', 1, 1, -1), ('x', 1, 0, 1), ('x', 1, 0, -1), ('rs', 0, 2, -1), ('rs', 0, 3, 1),
    ('z', 0, 3, 1), ('rs', 1, 3, 1), ('x', 0, 0, 1), ('rs', 1, 2, -1), ('z', 1, 2, 1), ('z', 0, 3, -1),
    ('z', 1, 2, -1), ('x', 0, 3, -1), ('x', 0, -1, -1), ('x', 0, 1, 1), ('cross', 0), ('fz', 0), ('x', 0, -3, -1),
    ('x', 0, -3, 1), ('x', 0, 1, -1), ('cross', 1), ('x', 1, 1, 1), ('x', 0, -2, 1), ('z', 1, 3, -1),
    ('z', 1, 3, 1), ('ag', 0, 0, 1), ('x', 0, 0, -1), ('x', 0, -1, 1), ('x', 0, 2, -1), ('x', 1, -1, 1),
    ('x', 1, 1, -1), ('fz', 1), ('ag', 1, 0, -1), ('c', 0, 1, -1), ('ag', 1, 0, 1), ('x', 0, -2, -1),
    ('c', 0, 1, 1), ('x', 1, -1, -1), ('ag', 0, 0, -1), ('ag', 0, 1, 1), ('x', 1, 2, -1), ('c', 1, 1, -1),
    ('x', 0, 2, 1), ('ag', 1, 1, 1), ('ag', 1, 1, -1), ('x', 1, -2, -1), ('c', 1, 1, 1), ('ag', 0, 2, 1),
    ('x', 0, 3, 1), ('ag', 0, 1, -1), ('x', 1, 2, 1), ('c', 0, 2, 1), ('c', 0, 2, -1), ('x', 1, -3, 1),
    ('ag', 1, 2, 1), ('ag', 0, 2, -1), ('c', 1, 2, 1), ('x', 1, -3, -1), ('c', 1, 2, -1), ('x', 1, -2, 1),
    ('ag', 1, 2, -1), ('x', 1, 3, -1), ('x', 1, 3, 1), ('ag', 0, 3, 1), ('ag', 1, 3, 1),
)


class Copy:
    def __init__(self, src, dst, landing, send, recv, device, sends=None, receives=None):
        self.out = (src, dst, send, recv, device)
        self.into = (landing, landing, send, recv, device)
        self.sends, self.receives = sends, receives

    def start(self):
        guarded(self.sends, lambda: remote(*self.out).start())

    def wait_recv(self):
        guarded(self.receives, lambda: remote(*self.into).wait_recv())

    def wait_send(self):
        guarded(self.sends, lambda: remote(*self.out).wait_send())


def remote(src, dst, send, recv, device):
    return pltpu.make_async_remote_copy(
        src_ref=src, dst_ref=dst, send_sem=send, recv_sem=recv, device_id=device, device_id_type=MESH
    )


def guarded(condition, action):
    if condition is None:
        action()
    else:
        pl.when(condition)(action)


def multiply(k, occ_ref, pair_ref, first, panel, held, out_ref):
    positions = pair_ref.shape[1]
    slots = panel.shape[1] // out_ref.shape[0]
    bf, f32 = jnp.bfloat16, jnp.float32

    def split(value):
        high = value.astype(bf)
        return high, (value - high.astype(f32)).astype(bf)

    def one(o, carry):
        label = occ_ref[first + o]
        here = pl.ds(pl.multiple_of(o * TILE, TILE), TILE)
        count = jnp.int32(0)
        index = [jnp.int32(0)] * slots
        for t in range(positions):
            match = pair_ref[k, t] == label
            for s in range(min(slots, t + 1)):
                index[s] = jnp.where(match & (count == s), t, index[s])
            count = count + match.astype(jnp.int32)
        total = None if k == 0 else out_ref[here, :]
        for pair in range(slots // 2):
            left, right = [], []
            for s in (2 * pair, 2 * pair + 1):
                rows = pl.multiple_of((o * slots + s) * TILE, TILE)
                tile = panel[k, pl.ds(rows, TILE), :]
                left.append(jnp.where(count > s, tile, 0.0))
                right.append(held[index[s] // NZ, index[s] % NZ])
            a_high, a_low = split(jnp.concatenate(left, axis=1))
            b_high, b_low = split(jnp.concatenate(right, axis=0))
            dot = functools.partial(jnp.dot, preferred_element_type=f32)
            part = dot(a_high, b_high) + (dot(a_high, b_low) + dot(a_low, b_high))
            total = part if total is None else total + part
        out_ref[here, :] = total
        return carry

    lax.fori_loop(0, out_ref.shape[0] // TILE, one, 0)


def kernel(owner_ref, occ_ref, pair_ref, amp_ref, int_ref, out_ref, held_0, held_1, panel, both, right_out, right_in,
           left_out, left_in, mine_out, other_in, local_sem, z_sem, x_sem, xf_sem, xz_sem, rs_sem, ag_sem, sib_sem,
           cross_sem):
    row, col = lax.axis_index("row"), lax.axis_index("col")
    x, z = row // NZ, row % NZ
    y, h, c = col // (NH * NC), (col // NC) % NH, col % NC

    def device(dx=0, dz=0, dy=0, flip_h=False, flip_c=False):
        h2 = 1 - h if flip_h else h
        c2 = 1 - c if flip_c else c
        return (((x + dx + NX) % NX) * NZ + z + dz, ((y + dy + NY) % NY) * (NH * NC) + h2 * NC + c2)

    held = (held_0, held_1)
    sections = int_ref.shape[0]
    half = amp_ref.shape[0] // NC
    share = half // NY
    events, last, sent = {}, [[] for _ in range(sections)], []

    def go(copy):
        copy.start()
        sent.append(copy)

    barrier = pltpu.get_barrier_semaphore()
    partners = [device(dx=1), device(dx=-1), device(dy=1), device(dy=-1), device(flip_h=True), device(flip_c=True)]
    for partner in partners:
        pl.semaphore_signal(barrier, inc=1, device_id=partner, device_id_type=MESH)

    @pl.when(z > 0)
    def _():
        pl.semaphore_signal(barrier, inc=1, device_id=device(dz=-1), device_id_type=MESH)

    @pl.when(z < NZ - 1)
    def _():
        pl.semaphore_signal(barrier, inc=1, device_id=device(dz=1), device_id_type=MESH)

    own_ints = [pltpu.make_async_copy(int_ref.at[k], held[k].at[x, z], local_sem.at[1 + k]) for k in range(sections)]
    own_half = pltpu.make_async_copy(
        amp_ref.at[pl.ds(pl.multiple_of(c * half, 8), half), :], both.at[c], local_sem.at[0])
    for copy in own_ints:
        copy.start()
    own_half.start()
    pl.semaphore_wait(barrier, len(partners) + (z > 0).astype(jnp.int32) + (z < NZ - 1).astype(jnp.int32))

    mid = [(TILE - first) // 16 * 8 for first in X_ROWS]
    zr = [pl.ds(first, TILE - first) for first in X_ROWS]
    low = [pl.ds(first, m) for first, m in zip(X_ROWS, mid)]
    high = [pl.ds(first + m, TILE - first - m) for first, m in zip(X_ROWS, mid)]

    def z_copy(k, s, way):
        src = int_ref.at[k, zr[k]] if s == 1 else held[k].at[x, z - way * (s - 1), zr[k]]
        to = held[k].at[x, z - way * (s - 1), zr[k]]
        frm = held[k].at[x, z - way * s, zr[k]]
        if way > 0:
            sends, receives = (z < NZ - 1) & (z - (s - 1) >= 0), z - s >= 0
        else:
            sends, receives = (z > 0) & (z + (s - 1) <= NZ - 1), z + s <= NZ - 1
        w = 0 if way > 0 else 1
        return Copy(src, to, frm, z_sem.at[0, k, s - 1, w], z_sem.at[1, k, s - 1, w], device(dz=way), sends, receives)

    def x_copy(k, d, way):
        zz = z + d
        valid = None if d == 0 else (zz >= 0) & (zz <= NZ - 1)
        src = int_ref.at[k, zr[k]] if d == 0 else held[k].at[x, zz, zr[k]]
        w = 0 if way > 0 else 1
        return Copy(src, held[k].at[x, zz, zr[k]], held[k].at[(x - way + NX) % NX, zz, zr[k]],
                    x_sem.at[0, k, zz, w], x_sem.at[1, k, zz, w], device(dx=way), valid, valid)

    def x_forward(k, d, way):
        zz = z + d
        valid = None if d == 0 else (zz >= 0) & (zz <= NZ - 1)
        rows = low[k] if way > 0 else high[k]
        xs = (x - way + NX) % NX
        w = 2 if way > 0 else 3
        return Copy(held[k].at[xs, zz, rows], held[k].at[xs, zz, rows], held[k].at[(x + 2) % NX, zz, rows],
                    x_sem.at[0, k, zz, w], x_sem.at[1, k, zz, w], device(dx=way), valid, valid)

    for k in range(sections):
        for d in OFFSETS:
            if d:
                way, s = (1, -d) if d < 0 else (-1, d)

                def arrived(k=k, d=d, way=way, s=s):
                    z_copy(k, s, way).wait_recv()
                    if s < NZ - 1:
                        go(z_copy(k, s + 1, way))
                    for side in (1, -1):
                        go(x_copy(k, d, side))

                events["z", k, s, way] = arrived
            for way in (1, -1):

                def passed(k=k, d=d, way=way):
                    x_copy(k, d, way).wait_recv()
                    go(x_forward(k, d, way))

                events["x", k, d, way] = passed
                last[k].append(x_forward(k, d, way))

    cut = [first // 16 * 8 for first in X_ROWS]
    xr = [pl.ds(0, first) for first in X_ROWS]
    xlow = [pl.ds(0, m) for m in cut]
    xhigh = [pl.ds(m, first - m) for first, m in zip(X_ROWS, cut)]

    def f_copy(k, way):
        w = 0 if way > 0 else 1
        return Copy(int_ref.at[k, xr[k]], held[k].at[x, z, xr[k]], held[k].at[(x - way + NX) % NX, z, xr[k]],
                    xf_sem.at[0, k, w], xf_sem.at[1, k, w], device(dx=way))

    def f_forward(k, way):
        rows = xlow[k] if way > 0 else xhigh[k]
        xs = (x - way + NX) % NX
        w = 2 if way > 0 else 3
        return Copy(held[k].at[xs, z, rows], held[k].at[xs, z, rows], held[k].at[(x + 2) % NX, z, rows],
                    xf_sem.at[0, k, w], xf_sem.at[1, k, w], device(dx=way))

    def fz_copy(k, s, way):
        to = held[k].at[:, z - way * (s - 1), xr[k]]
        frm = held[k].at[:, z - way * s, xr[k]]
        if way > 0:
            sends, receives = (z < NZ - 1) & (z - (s - 1) >= 0), z - s >= 0
        else:
            sends, receives = (z > 0) & (z + (s - 1) <= NZ - 1), z + s <= NZ - 1
        w = 0 if way > 0 else 1
        return Copy(to, to, frm, xz_sem.at[0, k, s - 1, w], xz_sem.at[1, k, s - 1, w], device(dz=way), sends, receives)

    for k in range(sections):

        def spread(k=k):
            for way in (1, -1):
                go(f_copy(k, way))

        events["fs", k] = spread
        for way in (1, -1):

            def near(k=k, way=way):
                f_copy(k, way).wait_recv()
                go(f_forward(k, way))

            events["f", k, way] = near
            for s in range(1, NZ - 1):

                def climb(k=k, s=s, way=way):
                    fz_copy(k, s, way).wait_recv()
                    go(fz_copy(k, s + 1, way))

                events["c", k, s, way] = climb
            last[k].append(fz_copy(k, NZ - 1, way))

        def far(k=k):
            own_ints[k].wait()
            for way in (1, -1):
                f_forward(k, way).wait_recv()
            for way in (1, -1):
                go(fz_copy(k, 1, way))

        events["fz", k] = far

    def half_rows(core):
        return pl.ds(pl.multiple_of(core * half, 8), half)

    swap = Copy(amp_ref.at[half_rows(1 - c), :], both.at[c], both.at[1 - c], sib_sem.at[0, sections, 0],
                sib_sem.at[1, sections, 0], device(flip_c=True))

    owner_y = [owner_ref[k] // (NH * NC) for k in range(sections)]
    owner_h = [(owner_ref[k] // NC) % NH for k in range(sections)]
    owner_c = [owner_ref[k] % NC for k in range(sections)]

    def stored(k, j):
        rows = pl.ds(pl.multiple_of(j * share, 8), share)
        return jnp.where(owner_c[k] == 0, both[0, rows, :], both[1, rows, :])

    def rs_copy(k, i, way):
        w = 0 if way > 0 else 1
        src, dst = (right_out, right_in) if way > 0 else (left_out, left_in)
        return Copy(src.at[k, i], dst.at[k, i], dst.at[k, i], rs_sem.at[0, k, i, w], rs_sem.at[1, k, i, w], device(dy=way))

    def rs_send(k, i, way):
        j = (y + 4 - i) % NY if way > 0 else (y - 3 + i + NY) % NY
        src, dst = (right_out, right_in) if way > 0 else (left_out, left_in)
        value = stored(k, j)
        if i:
            value = jnp.where(owner_y[k] == y, value, dst[k, i - 1])
        src[k, i] = value
        go(rs_copy(k, i, way))

    def cross_copy(k):
        return Copy(mine_out.at[k], other_in.at[k], other_in.at[k], cross_sem.at[0, k], cross_sem.at[1, k],
                    device(flip_h=True))

    def share_rows(j, core):
        return pl.ds(pl.multiple_of(core * half + j * share, 8), share)

    def ag_copy(k, i, way):
        j = (y - way * i + NY) % NY
        g = (y - way * (i + 1) + NY) % NY
        w = 0 if way > 0 else 1
        return Copy(panel.at[k, share_rows(j, c), :], panel.at[k, share_rows(j, c), :], panel.at[k, share_rows(g, c), :],
                    ag_sem.at[0, k, i, w], ag_sem.at[1, k, i, w], device(dy=way))

    def sib_copy(k, d):
        j = (y - d + NY) % NY
        n = d + 3
        return Copy(panel.at[k, share_rows(j, c), :], panel.at[k, share_rows(j, c), :], panel.at[k, share_rows(j, 1 - c), :],
                    sib_sem.at[0, k, n], sib_sem.at[1, k, n], device(flip_c=True))

    def swapped():
        own_half.wait()
        swap.wait_recv()
        for k in range(sections):
            for way in (1, -1):
                rs_send(k, 0, way)

    events["swap",] = swapped
    steps = {1: NY // 2, -1: NY // 2 - 1}
    for k in range(sections):
        ended = []
        for way in (1, -1):
            for i in range(steps[way]):

                def advance(k=k, i=i, way=way, ended=ended):
                    rs_copy(k, i, way).wait_recv()
                    if i < steps[way] - 1:
                        rs_send(k, i + 1, way)
                    else:
                        ended.append(way)
                    if len(ended) == 2:
                        ended.append(0)
                        ahead = (owner_y[k] - y + NY) % NY
                        mine_out[k] = jnp.where(
                            ahead == 0, stored(k, y), jnp.where(ahead <= 3, left_in[k, 2], right_in[k, 3]))
                        go(cross_copy(k))

                def gathered(k=k, i=i, way=way):
                    ag_copy(k, i, way).wait_recv()
                    if i < steps[way] - 1:
                        go(ag_copy(k, i + 1, way))
                    go(sib_copy(k, way * (i + 1)))

                events["rs", k, i, way] = advance
                events["ag", k, i, way] = gathered

        def crossed(k=k):
            cross_copy(k).wait_recv()
            panel[k, share_rows(y, c), :] = jnp.where(owner_h[k] == h, mine_out[k], other_in[k])
            for way in (1, -1):
                go(ag_copy(k, 0, way))
            go(sib_copy(k, 0))

        events["cross", k] = crossed
        last[k].extend(sib_copy(k, d) for d in range(-3, 5))

    go(swap)
    for k in range(sections):
        for way in (1, -1):
            go(z_copy(k, 1, way))
        for way in (1, -1):
            go(x_copy(k, 0, way))
    for key in ORDER:
        events.pop(key)()
    assert not events
    for k in range(sections):
        for copy in last[k]:
            copy.wait_recv()
        multiply(k, occ_ref, pair_ref, row * (out_ref.shape[0] // TILE), panel, held[k], out_ref)
    for copy in sent:
        copy.wait_send()


def on_device(amplitudes, integrals, owner_column, occ_irrep, pair_irrep):
    tiles_here, slots, tile = amplitudes.shape[1:4]
    sections, _, columns = integrals.shape
    rows = tiles_here * slots * tile
    half, share = rows // NC, rows // NC // NY
    f32 = jnp.float32
    dma = pltpu.SemaphoreType.DMA
    smem = pl.BlockSpec(memory_space=pltpu.SMEM)
    return pl.pallas_call(
        kernel,
        out_shape=jax.ShapeDtypeStruct((tiles_here * tile, columns), f32),
        in_specs=[smem, smem, smem, pl.BlockSpec(memory_space=pl.ANY), pl.BlockSpec(memory_space=pl.ANY)],
        out_specs=pl.BlockSpec(memory_space=pltpu.VMEM),
        scratch_shapes=[
            pltpu.VMEM((NX, NZ, tile, columns), f32),
            pltpu.VMEM((NX, NZ, tile, columns), f32),
            pltpu.VMEM((sections, rows, tile), f32),
            pltpu.VMEM((NC, half, tile), f32),
            pltpu.VMEM((sections, 4, share, tile), f32),
            pltpu.VMEM((sections, 4, share, tile), f32),
            pltpu.VMEM((sections, 3, share, tile), f32),
            pltpu.VMEM((sections, 3, share, tile), f32),
            pltpu.VMEM((sections, share, tile), f32),
            pltpu.VMEM((sections, share, tile), f32),
            dma((1 + sections,)),
            dma((2, sections, 3, 2)),
            dma((2, sections, 4, 4)),
            dma((2, sections, 4)),
            dma((2, sections, 3, 2)),
            dma((2, sections, 4, 2)),
            dma((2, sections, 4, 2)),
            dma((2, sections + 1, 8)),
            dma((2, sections)),
        ],
        compiler_params=pltpu.CompilerParams(
            collective_id=0, has_side_effects=True, vmem_limit_bytes=48 * 1024 * 1024
        ),
        name="ladder",
    )(*(pltpu.with_memory_space_constraint(v, pltpu.HBM)
        for v in (owner_column, occ_irrep, pair_irrep, amplitudes.reshape(rows, tile), integrals)))


def solution(mesh):
    return jax.shard_map(
        on_device,
        mesh=mesh,
        in_specs=(P("col", "row", None, None, None), P(None, "row", "col"), P(), P(), P()),
        out_specs=P("row", "col"),
        check_vma=False,
    )
```

```python
import functools

import jax
import jax.numpy as jnp
from jax import lax
from jax.experimental import pallas as pl
from jax.experimental.pallas import tpu as pltpu
from jax.sharding import PartitionSpec as P

MESH = pl.DeviceIdType.MESH
NX, NZ, NY, NH, NC = 4, 4, 8, 2, 2
TILE = 128
X_ROWS = (24, 16)
OFFSETS = (0, -1, 1, -2, 2, -3, 3)
ORDER = (
    ('swap',), ('fs', 0), ('fs', 1), ('z', 0, 1, -1), ('z', 0, 1, 1), ('rs', 0, 0, 1), ('rs', 1, 0, 1),
    ('z', 1, 1, 1), ('z', 1, 1, -1), ('rs', 0, 0, -1), ('rs', 1, 0, -1), ('f', 0, -1), ('rs', 0, 1, 1),
    ('rs', 1, 1, 1), ('z', 0, 2, 1), ('rs', 0, 1, -1), ('z', 0, 2, -1), ('f', 0, 1), ('rs', 0, 2, 1),
    ('rs', 1, 1, -1), ('rs', 1, 2, 1), ('x', 0, 0, 1), ('rs', 0, 2, -1), ('x', 0, 0, -1), ('f', 1, -1),
    ('rs', 0, 3, 1), ('z', 0, 3, -1), ('rs', 1, 2, -1), ('f', 1, 1), ('rs', 1, 3, 1), ('x', 1, 0, -1),
    ('z', 1, 2, -1), ('x', 0, 1, -1), ('z', 1, 2, 1), ('x', 1, 0, 1), ('cross', 0), ('x', 0, 1, 1), ('fz', 0),
    ('z', 0, 3, 1), ('cross', 1), ('x', 0, -1, -1), ('ag', 0, 0, 1), ('z', 1, 3, 1), ('fz', 1), ('z', 1, 3, -1),
    ('x', 1, -1, -1), ('x', 0, 2, 1), ('ag', 0, 0, -1), ('x', 0, -2, -1), ('x', 0, 3, 1), ('ag', 1, 0, 1),
    ('ag', 1, 0, -1), ('x', 0, -1, 1), ('c', 0, 1, -1), ('c', 0, 1, 1), ('x', 0, 2, -1), ('ag', 0, 1, 1),
    ('x', 1, 1, -1), ('x', 0, -2, 1), ('x', 0, -3, -1), ('ag', 0, 1, -1), ('x', 1, 2, 1), ('ag', 1, 1, 1),
    ('x', 1, -3, 1), ('x', 1, 1, 1), ('x', 0, -3, 1), ('x', 1, -1, 1), ('ag', 1, 1, -1), ('c', 1, 1, 1),
    ('x', 1, -3, -1), ('c', 1, 1, -1), ('x', 0, 3, -1), ('ag', 0, 2, 1), ('c', 0, 2, -1), ('c', 0, 2, 1),
    ('x', 1, 3, -1), ('ag', 1, 2, 1), ('c', 1, 2, 1), ('ag', 0, 2, -1), ('c', 1, 2, -1), ('x', 1, 2, -1),
    ('ag', 0, 3, 1), ('x', 1, 3, 1), ('x', 1, -2, 1), ('ag', 1, 2, -1), ('x', 1, -2, -1), ('ag', 1, 3, 1),
)


class Copy:
    def __init__(self, src, dst, landing, send, recv, device, sends=None, receives=None):
        self.out = (src, dst, send, recv, device)
        self.into = (landing, landing, send, recv, device)
        self.sends, self.receives = sends, receives

    def start(self):
        guarded(self.sends, lambda: remote(*self.out).start())

    def wait_recv(self):
        guarded(self.receives, lambda: remote(*self.into).wait_recv())

    def wait_send(self):
        guarded(self.sends, lambda: remote(*self.out).wait_send())


def remote(src, dst, send, recv, device):
    return pltpu.make_async_remote_copy(
        src_ref=src, dst_ref=dst, send_sem=send, recv_sem=recv, device_id=device, device_id_type=MESH
    )


def guarded(condition, action):
    if condition is None:
        action()
    else:
        pl.when(condition)(action)


def find_slots(k, occ_ref, pair_ref, first, index_ref, count_ref):
    positions, tiles = pair_ref.shape[1], count_ref.shape[0] // pair_ref.shape[0]
    slots = index_ref.shape[0] // count_ref.shape[0]

    def one(o, carry):
        label = occ_ref[first + o]
        count = jnp.int32(0)
        index = [jnp.int32(0)] * slots
        for t in range(positions):
            match = pair_ref[k, t] == label
            for s in range(min(slots, t + 1)):
                index[s] = jnp.where(match & (count == s), t, index[s])
            count = count + match.astype(jnp.int32)
        for s in range(slots):
            index_ref[(k * tiles + o) * slots + s] = index[s]
        count_ref[k * tiles + o] = count
        return carry

    lax.fori_loop(0, tiles, one, 0)


def multiply(k, index_ref, count_ref, panel, held, out_ref):
    tiles = out_ref.shape[0] // TILE
    slots = panel.shape[1] // out_ref.shape[0]
    bf, f32 = jnp.bfloat16, jnp.float32
    dot = functools.partial(jnp.dot, preferred_element_type=f32)

    def split(value):
        high = value.astype(bf)
        return high, (value - high.astype(f32)).astype(bf)

    def one(o, carry):
        here = pl.ds(pl.multiple_of(o * TILE, TILE), TILE)
        count = count_ref[k * tiles + o]
        total = None if k == 0 else out_ref[here, :]
        for pair in range(slots // 2):
            left, right = [], []
            for s in (2 * pair, 2 * pair + 1):
                rows = pl.multiple_of((o * slots + s) * TILE, TILE)
                tile = panel[k, pl.ds(rows, TILE), :]
                left.append(jnp.where(count > s, tile, 0.0))
                t = index_ref[(k * tiles + o) * slots + s]
                right.append(held[t // NZ, t % NZ])
            a_high, a_low = split(jnp.concatenate(left, axis=1))
            b_high, b_low = split(jnp.concatenate(right, axis=0))
            both = dot(jnp.concatenate([a_high, a_low], axis=0), b_high)
            part = both[:TILE] + (both[TILE:] + dot(a_high, b_low))
            total = part if total is None else total + part
        out_ref[here, :] = total
        return carry

    lax.fori_loop(0, tiles, one, 0)


def kernel(owner_hbm, occ_hbm, pair_hbm, amp_ref, int_ref, out_ref, owner_ref, occ_ref, pair_ref, index_ref, count_ref,
           held_0, held_1, panel, both, right_out, right_in,
           left_out, left_in, mine_out, other_in, local_sem, z_sem, x_sem, xf_sem, xz_sem, rs_sem, ag_sem, sib_sem,
           cross_sem, ready_sem):
    row, col = lax.axis_index("row"), lax.axis_index("col")
    x, z = row // NZ, row % NZ
    y, h, c = col // (NH * NC), (col // NC) % NH, col % NC

    def device(dx=0, dz=0, dy=0, flip_h=False, flip_c=False):
        h2 = 1 - h if flip_h else h
        c2 = 1 - c if flip_c else c
        return (((x + dx + NX) % NX) * NZ + z + dz, ((y + dy + NY) % NY) * (NH * NC) + h2 * NC + c2)

    held = (held_0, held_1)
    sections = int_ref.shape[0]
    half = amp_ref.shape[0] // NC
    share = half // NY
    events, last, sent = {}, [[] for _ in range(sections)], []

    def go(copy):
        copy.start()
        sent.append(copy)

    barrier = pltpu.get_barrier_semaphore()
    greets_up, greets_down, greets_h = y < NY // 2, (y == 0) | (y > NY // 2), h == 0
    waits_up, waits_down, waits_h = y >= NY // 2, (y > 0) & (y <= NY // 2), h == 1

    def greet(partner, condition=None):
        guarded(condition, lambda: pl.semaphore_signal(barrier, inc=1, device_id=partner, device_id_type=MESH))

    greet(device(dx=1))
    greet(device(dx=-1))
    greet(device(flip_c=True))
    greet(device(dz=-1), z > 0)
    greet(device(dz=1), z < NZ - 1)
    greet(device(dy=1), greets_up)
    greet(device(dy=-1), greets_down)
    greet(device(flip_h=True), greets_h)
    peers = jnp.int32(3)
    for condition in (z > 0, z < NZ - 1, waits_up, waits_down, waits_h):
        peers = peers + condition.astype(jnp.int32)

    def answer(n, partner, condition):
        guarded(condition, lambda: pl.semaphore_signal(
            ready_sem.at[n], inc=1, device_id=partner, device_id_type=MESH))

    def answered(n, condition):
        guarded(condition, lambda: pl.semaphore_wait(ready_sem.at[n], 1))

    own_ints = [pltpu.make_async_copy(int_ref.at[k], held[k].at[x, z], local_sem.at[1 + k]) for k in range(sections)]
    labels = [
        pltpu.make_async_copy(src, dst, local_sem.at[1 + sections + n])
        for n, (src, dst) in enumerate(((owner_hbm, owner_ref), (occ_hbm, occ_ref), (pair_hbm, pair_ref)))
    ]
    own_half = pltpu.make_async_copy(
        amp_ref.at[pl.ds(pl.multiple_of(c * half, 8), half), :], both.at[c], local_sem.at[0])
    for copy in (*labels, *own_ints):
        copy.start()
    own_half.start()
    pl.semaphore_wait(barrier, peers)
    answer(1, device(dy=1), waits_up)
    answer(0, device(dy=-1), waits_down)
    answer(2, device(flip_h=True), waits_h)

    mid = [(TILE - first) // 16 * 8 for first in X_ROWS]
    zr = [pl.ds(first, TILE - first) for first in X_ROWS]
    low = [pl.ds(first, m) for first, m in zip(X_ROWS, mid)]
    high = [pl.ds(first + m, TILE - first - m) for first, m in zip(X_ROWS, mid)]

    def z_copy(k, s, way):
        src = int_ref.at[k, zr[k]] if s == 1 else held[k].at[x, z - way * (s - 1), zr[k]]
        to = held[k].at[x, z - way * (s - 1), zr[k]]
        frm = held[k].at[x, z - way * s, zr[k]]
        if way > 0:
            sends, receives = (z < NZ - 1) & (z - (s - 1) >= 0), z - s >= 0
        else:
            sends, receives = (z > 0) & (z + (s - 1) <= NZ - 1), z + s <= NZ - 1
        w = 0 if way > 0 else 1
        return Copy(src, to, frm, z_sem.at[0, k, s - 1, w], z_sem.at[1, k, s - 1, w], device(dz=way), sends, receives)

    def x_copy(k, d, way):
        zz = z + d
        valid = None if d == 0 else (zz >= 0) & (zz <= NZ - 1)
        src = int_ref.at[k, zr[k]] if d == 0 else held[k].at[x, zz, zr[k]]
        w = 0 if way > 0 else 1
        return Copy(src, held[k].at[x, zz, zr[k]], held[k].at[(x - way + NX) % NX, zz, zr[k]],
                    x_sem.at[0, k, zz, w], x_sem.at[1, k, zz, w], device(dx=way), valid, valid)

    def x_forward(k, d, way):
        zz = z + d
        valid = None if d == 0 else (zz >= 0) & (zz <= NZ - 1)
        rows = low[k] if way > 0 else high[k]
        xs = (x - way + NX) % NX
        w = 2 if way > 0 else 3
        return Copy(held[k].at[xs, zz, rows], held[k].at[xs, zz, rows], held[k].at[(x + 2) % NX, zz, rows],
                    x_sem.at[0, k, zz, w], x_sem.at[1, k, zz, w], device(dx=way), valid, valid)

    for k in range(sections):
        for d in OFFSETS:
            if d:
                way, s = (1, -d) if d < 0 else (-1, d)

                def arrived(k=k, d=d, way=way, s=s):
                    z_copy(k, s, way).wait_recv()
                    if s < NZ - 1:
                        go(z_copy(k, s + 1, way))
                    for side in (1, -1):
                        go(x_copy(k, d, side))

                events["z", k, s, way] = arrived
            for way in (1, -1):

                def passed(k=k, d=d, way=way):
                    x_copy(k, d, way).wait_recv()
                    go(x_forward(k, d, way))

                events["x", k, d, way] = passed
                last[k].append(x_forward(k, d, way))

    cut = [first // 16 * 8 for first in X_ROWS]
    xr = [pl.ds(0, first) for first in X_ROWS]
    xlow = [pl.ds(0, m) for m in cut]
    xhigh = [pl.ds(m, first - m) for first, m in zip(X_ROWS, cut)]

    def f_copy(k, way):
        w = 0 if way > 0 else 1
        return Copy(int_ref.at[k, xr[k]], held[k].at[x, z, xr[k]], held[k].at[(x - way + NX) % NX, z, xr[k]],
                    xf_sem.at[0, k, w], xf_sem.at[1, k, w], device(dx=way))

    def f_forward(k, way):
        rows = xlow[k] if way > 0 else xhigh[k]
        xs = (x - way + NX) % NX
        w = 2 if way > 0 else 3
        return Copy(held[k].at[xs, z, rows], held[k].at[xs, z, rows], held[k].at[(x + 2) % NX, z, rows],
                    xf_sem.at[0, k, w], xf_sem.at[1, k, w], device(dx=way))

    def fz_copy(k, s, way):
        to = held[k].at[:, z - way * (s - 1), xr[k]]
        frm = held[k].at[:, z - way * s, xr[k]]
        if way > 0:
            sends, receives = (z < NZ - 1) & (z - (s - 1) >= 0), z - s >= 0
        else:
            sends, receives = (z > 0) & (z + (s - 1) <= NZ - 1), z + s <= NZ - 1
        w = 0 if way > 0 else 1
        return Copy(to, to, frm, xz_sem.at[0, k, s - 1, w], xz_sem.at[1, k, s - 1, w], device(dz=way), sends, receives)

    for k in range(sections):

        def spread(k=k):
            for way in (1, -1):
                go(f_copy(k, way))

        events["fs", k] = spread
        for way in (1, -1):

            def near(k=k, way=way):
                f_copy(k, way).wait_recv()
                go(f_forward(k, way))

            events["f", k, way] = near
            for s in range(1, NZ - 1):

                def climb(k=k, s=s, way=way):
                    fz_copy(k, s, way).wait_recv()
                    go(fz_copy(k, s + 1, way))

                events["c", k, s, way] = climb
            last[k].append(fz_copy(k, NZ - 1, way))

        def far(k=k):
            own_ints[k].wait()
            for way in (1, -1):
                f_forward(k, way).wait_recv()
            for way in (1, -1):
                go(fz_copy(k, 1, way))

        events["fz", k] = far

    def half_rows(core):
        return pl.ds(pl.multiple_of(core * half, 8), half)

    swap = Copy(amp_ref.at[half_rows(1 - c), :], both.at[c], both.at[1 - c], sib_sem.at[0, sections, 0],
                sib_sem.at[1, sections, 0], device(flip_c=True))

    def owner(k):
        col_k = owner_ref[k]
        return col_k // (NH * NC), (col_k // NC) % NH, col_k % NC

    def stored(k, j):
        rows = pl.ds(pl.multiple_of(j * share, 8), share)
        return jnp.where(owner(k)[2] == 0, both[0, rows, :], both[1, rows, :])

    def rs_copy(k, i, way):
        w = 0 if way > 0 else 1
        src, dst = (right_out, right_in) if way > 0 else (left_out, left_in)
        return Copy(src.at[k, i], dst.at[k, i], dst.at[k, i], rs_sem.at[0, k, i, w], rs_sem.at[1, k, i, w], device(dy=way))

    def rs_send(k, i, way):
        j = (y + 4 - i) % NY if way > 0 else (y - 3 + i + NY) % NY
        src, dst = (right_out, right_in) if way > 0 else (left_out, left_in)
        value = stored(k, j)
        if i:
            value = jnp.where(owner(k)[0] == y, value, dst[k, i - 1])
        src[k, i] = value
        go(rs_copy(k, i, way))

    def cross_copy(k):
        return Copy(mine_out.at[k], other_in.at[k], other_in.at[k], cross_sem.at[0, k], cross_sem.at[1, k],
                    device(flip_h=True))

    def share_rows(j, core):
        return pl.ds(pl.multiple_of(core * half + j * share, 8), share)

    def ag_copy(k, i, way):
        j = (y - way * i + NY) % NY
        g = (y - way * (i + 1) + NY) % NY
        w = 0 if way > 0 else 1
        return Copy(panel.at[k, share_rows(j, c), :], panel.at[k, share_rows(j, c), :], panel.at[k, share_rows(g, c), :],
                    ag_sem.at[0, k, i, w], ag_sem.at[1, k, i, w], device(dy=way))

    def sib_copy(k, d):
        j = (y - d + NY) % NY
        n = d + 3
        return Copy(panel.at[k, share_rows(j, c), :], panel.at[k, share_rows(j, c), :], panel.at[k, share_rows(j, 1 - c), :],
                    sib_sem.at[0, k, n], sib_sem.at[1, k, n], device(flip_c=True))

    def swapped():
        own_half.wait()
        swap.wait_recv()
        answered(0, greets_up)
        answered(1, greets_down)
        for k in range(sections):
            for way in (1, -1):
                rs_send(k, 0, way)

    events["swap",] = swapped
    crossing = []
    steps = {1: NY // 2, -1: NY // 2 - 1}
    for k in range(sections):
        ended = []
        for way in (1, -1):
            for i in range(steps[way]):

                def advance(k=k, i=i, way=way, ended=ended):
                    rs_copy(k, i, way).wait_recv()
                    if i < steps[way] - 1:
                        rs_send(k, i + 1, way)
                    else:
                        ended.append(way)
                    if len(ended) == 2:
                        ended.append(0)
                        ahead = (owner(k)[0] - y + NY) % NY
                        mine_out[k] = jnp.where(
                            ahead == 0, stored(k, y), jnp.where(ahead <= 3, left_in[k, 2], right_in[k, 3]))
                        if not crossing:
                            crossing.append(k)
                            answered(2, greets_h)
                        go(cross_copy(k))

                def gathered(k=k, i=i, way=way):
                    ag_copy(k, i, way).wait_recv()
                    if i < steps[way] - 1:
                        go(ag_copy(k, i + 1, way))
                    go(sib_copy(k, way * (i + 1)))

                events["rs", k, i, way] = advance
                events["ag", k, i, way] = gathered

        def crossed(k=k):
            cross_copy(k).wait_recv()
            panel[k, share_rows(y, c), :] = jnp.where(owner(k)[1] == h, mine_out[k], other_in[k])
            for way in (1, -1):
                go(ag_copy(k, 0, way))
            go(sib_copy(k, 0))

        events["cross", k] = crossed
        last[k].extend(sib_copy(k, d) for d in range(-3, 5))

    go(swap)
    for k in range(sections):
        for way in (1, -1):
            go(z_copy(k, 1, way))
        for way in (1, -1):
            go(x_copy(k, 0, way))
    for copy in labels:
        copy.wait()
    for k in range(sections):
        find_slots(k, occ_ref, pair_ref, row * (out_ref.shape[0] // TILE), index_ref, count_ref)
    for key in ORDER:
        events.pop(key)()
    assert not events
    for k in range(sections):
        if k == sections - 1:
            for copy in sent:
                copy.wait_send()
        for copy in last[k]:
            copy.wait_recv()
        multiply(k, index_ref, count_ref, panel, held[k], out_ref)


def on_device(amplitudes, integrals, owner_column, occ_irrep, pair_irrep):
    tiles_here, slots, tile = amplitudes.shape[1:4]
    sections, _, columns = integrals.shape
    rows = tiles_here * slots * tile
    half, share = rows // NC, rows // NC // NY
    f32 = jnp.float32
    dma = pltpu.SemaphoreType.DMA
    smem = functools.partial(pltpu.SMEM, dtype=jnp.int32)
    return pl.pallas_call(
        kernel,
        out_shape=jax.ShapeDtypeStruct((tiles_here * tile, columns), f32),
        in_specs=[pl.BlockSpec(memory_space=pl.ANY)] * 5,
        out_specs=pl.BlockSpec(memory_space=pltpu.VMEM),
        scratch_shapes=[
            smem(owner_column.shape),
            smem(occ_irrep.shape),
            smem(pair_irrep.shape),
            smem((sections * tiles_here * slots,)),
            smem((sections * tiles_here,)),
            pltpu.VMEM((NX, NZ, tile, columns), f32),
            pltpu.VMEM((NX, NZ, tile, columns), f32),
            pltpu.VMEM((sections, rows, tile), f32),
            pltpu.VMEM((NC, half, tile), f32),
            pltpu.VMEM((sections, 4, share, tile), f32),
            pltpu.VMEM((sections, 4, share, tile), f32),
            pltpu.VMEM((sections, 3, share, tile), f32),
            pltpu.VMEM((sections, 3, share, tile), f32),
            pltpu.VMEM((sections, share, tile), f32),
            pltpu.VMEM((sections, share, tile), f32),
            dma((4 + sections,)),
            dma((2, sections, 3, 2)),
            dma((2, sections, 4, 4)),
            dma((2, sections, 4)),
            dma((2, sections, 3, 2)),
            dma((2, sections, 4, 2)),
            dma((2, sections, 4, 2)),
            dma((2, sections + 1, 8)),
            dma((2, sections)),
            pltpu.SemaphoreType.REGULAR((3,)),
        ],
        compiler_params=pltpu.CompilerParams(
            collective_id=0, has_side_effects=True, vmem_limit_bytes=48 * 1024 * 1024
        ),
        name="ladder",
    )(*(pltpu.with_memory_space_constraint(v, pltpu.HBM)
        for v in (owner_column, occ_irrep, pair_irrep, amplitudes.reshape(rows, tile), integrals)))


def solution(mesh):
    return jax.shard_map(
        on_device,
        mesh=mesh,
        in_specs=(P("col", "row", None, None, None), P(None, "row", "col"), P(), P(), P()),
        out_specs=P("row", "col"),
        check_vma=False,
    )
```

```python
import functools

import jax
import jax.numpy as jnp
from jax import lax
from jax.experimental import pallas as pl
from jax.experimental.pallas import tpu as pltpu
from jax.sharding import PartitionSpec as P

MESH = pl.DeviceIdType.MESH
NX, NZ, NY, NH, NC = 4, 4, 8, 2, 2
TILE = 128
X_ROWS = (24, 24)
OFFSETS = (0, -1, 1, -2, 2, -3, 3)
ORDER = (
    ('swap',), ('fs', 0), ('fs', 1), ('z', 0, 1, 1), ('x', 0, 0, 1), ('z', 0, 1, -1), ('rs', 0, 0, 1),
    ('rs', 1, 0, 1), ('rs', 0, 0, -1), ('f', 0, -1), ('z', 1, 1, -1), ('z', 1, 1, 1), ('rs', 0, 1, 1),
    ('rs', 1, 0, -1), ('f', 1, -1), ('f', 0, 1), ('rs', 1, 1, 1), ('f', 1, 1), ('z', 0, 2, 1), ('z', 0, 2, -1),
    ('rs', 0, 1, -1), ('rs', 0, 2, 1), ('rs', 0, 2, -1), ('rs', 1, 1, -1), ('rs', 1, 2, 1), ('rs', 0, 3, 1),
    ('x', 0, 0, -1), ('rs', 1, 2, -1), ('rs', 1, 3, 1), ('z', 0, 3, 1), ('x', 0, -1, -1), ('z', 1, 2, 1),
    ('z', 1, 2, -1), ('x', 0, -3, -1), ('z', 0, 3, -1), ('x', 0, 1, -1), ('x', 0, -1, 1), ('x', 1, 0, 1), ('fz', 0),
    ('cross', 0), ('x', 0, 2, -1), ('x', 0, 1, 1), ('cross', 1), ('x', 0, 3, 1), ('fz', 1), ('ag', 0, 0, -1),
    ('ag', 0, 0, 1), ('x', 0, -2, 1), ('z', 1, 3, -1), ('x', 1, 0, -1), ('z', 1, 3, 1), ('c', 0, 1, 1),
    ('x', 0, 2, 1), ('x', 0, 3, -1), ('c', 0, 1, -1), ('ag', 1, 0, 1), ('ag', 1, 0, -1), ('x', 1, 1, 1),
    ('x', 1, 2, 1), ('ag', 0, 1, 1), ('x', 0, -2, -1), ('x', 1, -2, -1), ('c', 1, 1, -1), ('c', 1, 1, 1),
    ('x', 0, -3, 1), ('x', 1, 1, -1), ('ag', 1, 1, 1), ('x', 1, -1, -1), ('ag', 1, 1, -1), ('ag', 0, 1, -1),
    ('x', 1, -1, 1), ('c', 0, 2, 1), ('c', 0, 2, -1), ('ag', 0, 2, 1), ('x', 1, -3, -1), ('x', 1, 3, -1),
    ('x', 1, -2, 1), ('ag', 1, 2, 1), ('x', 1, 3, 1), ('c', 1, 2, 1), ('c', 1, 2, -1), ('x', 1, 2, -1),
    ('ag', 1, 2, -1), ('x', 1, -3, 1), ('ag', 0, 3, 1), ('ag', 0, 2, -1), ('ag', 1, 3, 1),
)


class Copy:
    def __init__(self, src, dst, landing, send, recv, device, sends=None, receives=None):
        self.out = (src, dst, send, recv, device)
        self.into = (landing, landing, send, recv, device)
        self.sends, self.receives = sends, receives

    def start(self):
        guarded(self.sends, lambda: remote(*self.out).start())

    def wait_recv(self):
        guarded(self.receives, lambda: remote(*self.into).wait_recv())

    def wait_send(self):
        guarded(self.sends, lambda: remote(*self.out).wait_send())


def remote(src, dst, send, recv, device):
    return pltpu.make_async_remote_copy(
        src_ref=src, dst_ref=dst, send_sem=send, recv_sem=recv, device_id=device, device_id_type=MESH
    )


def guarded(condition, action):
    if condition is None:
        action()
    else:
        pl.when(condition)(action)


def find_slots(k, occ_ref, pair_ref, first, index_ref, count_ref):
    positions, tiles = pair_ref.shape[1], count_ref.shape[0] // pair_ref.shape[0]
    slots = index_ref.shape[0] // count_ref.shape[0]

    def one(o, carry):
        label = occ_ref[first + o]
        count = jnp.int32(0)
        index = [jnp.int32(0)] * slots
        for t in range(positions):
            match = pair_ref[k, t] == label
            for s in range(min(slots, t + 1)):
                index[s] = jnp.where(match & (count == s), t, index[s])
            count = count + match.astype(jnp.int32)
        for s in range(slots):
            index_ref[(k * tiles + o) * slots + s] = index[s]
        count_ref[k * tiles + o] = count
        return carry

    lax.fori_loop(0, tiles, one, 0)


def multiply(k, index_ref, count_ref, panel, held, out_ref):
    tiles = out_ref.shape[0] // TILE
    slots = panel.shape[1] // out_ref.shape[0]
    bf, f32 = jnp.bfloat16, jnp.float32
    dot = functools.partial(jnp.dot, preferred_element_type=f32)

    def split(value):
        high = value.astype(bf)
        return high, (value - high.astype(f32)).astype(bf)

    def one(o, carry):
        here = pl.ds(pl.multiple_of(o * TILE, TILE), TILE)
        count = count_ref[k * tiles + o]
        total = None if k == 0 else out_ref[here, :]
        for pair in range(slots // 2):
            left, right = [], []
            for s in (2 * pair, 2 * pair + 1):
                rows = pl.multiple_of((o * slots + s) * TILE, TILE)
                tile = panel[k, pl.ds(rows, TILE), :]
                left.append(jnp.where(count > s, tile, 0.0))
                t = index_ref[(k * tiles + o) * slots + s]
                right.append(held[t // NZ, t % NZ])
            a_high, a_low = split(jnp.concatenate(left, axis=1))
            b_high, b_low = split(jnp.concatenate(right, axis=0))
            both = dot(jnp.concatenate([a_high, a_low], axis=0), b_high)
            part = both[:TILE] + (both[TILE:] + dot(a_high, b_low))
            total = part if total is None else total + part
        out_ref[here, :] = total
        return carry

    lax.fori_loop(0, tiles, one, 0, unroll=True)


def kernel(owner_hbm, occ_hbm, pair_hbm, amp_ref, int_ref, out_ref, owner_ref, occ_ref, pair_ref, index_ref, count_ref,
           held_0, held_1, panel, both, right_out, right_in,
           left_out, left_in, mine_out, other_in, local_sem, z_sem, x_sem, xf_sem, xz_sem, rs_sem, ag_sem, sib_sem,
           cross_sem, ready_sem):
    row, col = lax.axis_index("row"), lax.axis_index("col")
    x, z = row // NZ, row % NZ
    y, h, c = col // (NH * NC), (col // NC) % NH, col % NC

    def device(dx=0, dz=0, dy=0, flip_h=False, flip_c=False):
        h2 = 1 - h if flip_h else h
        c2 = 1 - c if flip_c else c
        return (((x + dx + NX) % NX) * NZ + z + dz, ((y + dy + NY) % NY) * (NH * NC) + h2 * NC + c2)

    held = (held_0, held_1)
    sections = int_ref.shape[0]
    half = amp_ref.shape[0] // NC
    share = half // NY
    events, last, sent = {}, [[] for _ in range(sections)], []

    def go(copy):
        copy.start()
        sent.append(copy)

    barrier = pltpu.get_barrier_semaphore()
    greets_up, greets_down, greets_h = y < NY // 2, (y == 0) | (y > NY // 2), h == 0
    waits_up, waits_down, waits_h = y >= NY // 2, (y > 0) & (y <= NY // 2), h == 1

    def greet(partner, condition=None):
        guarded(condition, lambda: pl.semaphore_signal(barrier, inc=1, device_id=partner, device_id_type=MESH))

    greet(device(dx=1))
    greet(device(dx=-1))
    greet(device(flip_c=True))
    greet(device(dz=-1), z > 0)
    greet(device(dz=1), z < NZ - 1)
    greet(device(dy=1), greets_up)
    greet(device(dy=-1), greets_down)
    greet(device(flip_h=True), greets_h)
    peers = jnp.int32(3)
    for condition in (z > 0, z < NZ - 1, waits_up, waits_down, waits_h):
        peers = peers + condition.astype(jnp.int32)

    def answer(n, partner, condition):
        guarded(condition, lambda: pl.semaphore_signal(
            ready_sem.at[n], inc=1, device_id=partner, device_id_type=MESH))

    def answered(n, condition):
        guarded(condition, lambda: pl.semaphore_wait(ready_sem.at[n], 1))

    own_ints = [pltpu.make_async_copy(int_ref.at[k], held[k].at[x, z], local_sem.at[1 + k]) for k in range(sections)]
    labels = [
        pltpu.make_async_copy(src, dst, local_sem.at[1 + sections + n])
        for n, (src, dst) in enumerate(((owner_hbm, owner_ref), (occ_hbm, occ_ref), (pair_hbm, pair_ref)))
    ]
    own_half = pltpu.make_async_copy(
        amp_ref.at[pl.ds(pl.multiple_of(c * half, 8), half), :], both.at[c], local_sem.at[0])
    for copy in (*labels, *own_ints):
        copy.start()
    own_half.start()
    pl.semaphore_wait(barrier, peers)
    answer(1, device(dy=1), waits_up)
    answer(0, device(dy=-1), waits_down)
    answer(2, device(flip_h=True), waits_h)

    mid = [(TILE - first) // 16 * 8 for first in X_ROWS]
    zr = [pl.ds(first, TILE - first) for first in X_ROWS]
    low = [pl.ds(first, m) for first, m in zip(X_ROWS, mid)]
    high = [pl.ds(first + m, TILE - first - m) for first, m in zip(X_ROWS, mid)]

    def z_copy(k, s, way):
        src = int_ref.at[k, zr[k]] if s == 1 else held[k].at[x, z - way * (s - 1), zr[k]]
        to = held[k].at[x, z - way * (s - 1), zr[k]]
        frm = held[k].at[x, z - way * s, zr[k]]
        if way > 0:
            sends, receives = (z < NZ - 1) & (z - (s - 1) >= 0), z - s >= 0
        else:
            sends, receives = (z > 0) & (z + (s - 1) <= NZ - 1), z + s <= NZ - 1
        w = 0 if way > 0 else 1
        return Copy(src, to, frm, z_sem.at[0, k, s - 1, w], z_sem.at[1, k, s - 1, w], device(dz=way), sends, receives)

    def x_copy(k, d, way):
        zz = z + d
        valid = None if d == 0 else (zz >= 0) & (zz <= NZ - 1)
        src = int_ref.at[k, zr[k]] if d == 0 else held[k].at[x, zz, zr[k]]
        w = 0 if way > 0 else 1
        return Copy(src, held[k].at[x, zz, zr[k]], held[k].at[(x - way + NX) % NX, zz, zr[k]],
                    x_sem.at[0, k, zz, w], x_sem.at[1, k, zz, w], device(dx=way), valid, valid)

    def x_forward(k, d, way):
        zz = z + d
        valid = None if d == 0 else (zz >= 0) & (zz <= NZ - 1)
        rows = low[k] if way > 0 else high[k]
        xs = (x - way + NX) % NX
        w = 2 if way > 0 else 3
        return Copy(held[k].at[xs, zz, rows], held[k].at[xs, zz, rows], held[k].at[(x + 2) % NX, zz, rows],
                    x_sem.at[0, k, zz, w], x_sem.at[1, k, zz, w], device(dx=way), valid, valid)

    for k in range(sections):
        for d in OFFSETS:
            if d:
                way, s = (1, -d) if d < 0 else (-1, d)

                def arrived(k=k, d=d, way=way, s=s):
                    z_copy(k, s, way).wait_recv()
                    if s < NZ - 1:
                        go(z_copy(k, s + 1, way))
                    for side in (1, -1):
                        go(x_copy(k, d, side))

                events["z", k, s, way] = arrived
            for way in (1, -1):

                def passed(k=k, d=d, way=way):
                    x_copy(k, d, way).wait_recv()
                    go(x_forward(k, d, way))

                events["x", k, d, way] = passed
                last[k].append(x_forward(k, d, way))

    cut = [first // 16 * 8 for first in X_ROWS]
    xr = [pl.ds(0, first) for first in X_ROWS]
    xlow = [pl.ds(0, m) for m in cut]
    xhigh = [pl.ds(m, first - m) for first, m in zip(X_ROWS, cut)]

    def f_copy(k, way):
        w = 0 if way > 0 else 1
        return Copy(int_ref.at[k, xr[k]], held[k].at[x, z, xr[k]], held[k].at[(x - way + NX) % NX, z, xr[k]],
                    xf_sem.at[0, k, w], xf_sem.at[1, k, w], device(dx=way))

    def f_forward(k, way):
        rows = xlow[k] if way > 0 else xhigh[k]
        xs = (x - way + NX) % NX
        w = 2 if way > 0 else 3
        return Copy(held[k].at[xs, z, rows], held[k].at[xs, z, rows], held[k].at[(x + 2) % NX, z, rows],
                    xf_sem.at[0, k, w], xf_sem.at[1, k, w], device(dx=way))

    def fz_copy(k, s, way):
        to = held[k].at[:, z - way * (s - 1), xr[k]]
        frm = held[k].at[:, z - way * s, xr[k]]
        if way > 0:
            sends, receives = (z < NZ - 1) & (z - (s - 1) >= 0), z - s >= 0
        else:
            sends, receives = (z > 0) & (z + (s - 1) <= NZ - 1), z + s <= NZ - 1
        w = 0 if way > 0 else 1
        return Copy(to, to, frm, xz_sem.at[0, k, s - 1, w], xz_sem.at[1, k, s - 1, w], device(dz=way), sends, receives)

    for k in range(sections):

        def spread(k=k):
            for way in (1, -1):
                go(f_copy(k, way))

        events["fs", k] = spread
        for way in (1, -1):

            def near(k=k, way=way):
                f_copy(k, way).wait_recv()
                go(f_forward(k, way))

            events["f", k, way] = near
            for s in range(1, NZ - 1):

                def climb(k=k, s=s, way=way):
                    fz_copy(k, s, way).wait_recv()
                    go(fz_copy(k, s + 1, way))

                events["c", k, s, way] = climb
            last[k].append(fz_copy(k, NZ - 1, way))

        def far(k=k):
            own_ints[k].wait()
            for way in (1, -1):
                f_forward(k, way).wait_recv()
            for way in (1, -1):
                go(fz_copy(k, 1, way))

        events["fz", k] = far

    def half_rows(core):
        return pl.ds(pl.multiple_of(core * half, 8), half)

    swap = Copy(amp_ref.at[half_rows(1 - c), :], both.at[c], both.at[1 - c], sib_sem.at[0, sections, 0],
                sib_sem.at[1, sections, 0], device(flip_c=True))

    def owner(k):
        col_k = owner_ref[k]
        return col_k // (NH * NC), (col_k // NC) % NH, col_k % NC

    def stored(k, j):
        rows = pl.ds(pl.multiple_of(j * share, 8), share)
        return jnp.where(owner(k)[2] == 0, both[0, rows, :], both[1, rows, :])

    def rs_copy(k, i, way):
        w = 0 if way > 0 else 1
        src, dst = (right_out, right_in) if way > 0 else (left_out, left_in)
        return Copy(src.at[k, i], dst.at[k, i], dst.at[k, i], rs_sem.at[0, k, i, w], rs_sem.at[1, k, i, w], device(dy=way))

    def rs_send(k, i, way):
        j = (y + 4 - i) % NY if way > 0 else (y - 3 + i + NY) % NY
        src, dst = (right_out, right_in) if way > 0 else (left_out, left_in)
        value = stored(k, j)
        if i:
            value = jnp.where(owner(k)[0] == y, value, dst[k, i - 1])
        src[k, i] = value
        go(rs_copy(k, i, way))

    def cross_copy(k):
        return Copy(mine_out.at[k], other_in.at[k], other_in.at[k], cross_sem.at[0, k], cross_sem.at[1, k],
                    device(flip_h=True))

    def share_rows(j, core):
        return pl.ds(pl.multiple_of(core * half + j * share, 8), share)

    def ag_copy(k, i, way):
        j = (y - way * i + NY) % NY
        g = (y - way * (i + 1) + NY) % NY
        w = 0 if way > 0 else 1
        return Copy(panel.at[k, share_rows(j, c), :], panel.at[k, share_rows(j, c), :], panel.at[k, share_rows(g, c), :],
                    ag_sem.at[0, k, i, w], ag_sem.at[1, k, i, w], device(dy=way))

    def sib_copy(k, d):
        j = (y - d + NY) % NY
        n = d + 3
        return Copy(panel.at[k, share_rows(j, c), :], panel.at[k, share_rows(j, c), :], panel.at[k, share_rows(j, 1 - c), :],
                    sib_sem.at[0, k, n], sib_sem.at[1, k, n], device(flip_c=True))

    def swapped():
        own_half.wait()
        swap.wait_recv()
        answered(0, greets_up)
        answered(1, greets_down)
        for k in range(sections):
            for way in (1, -1):
                rs_send(k, 0, way)

    events["swap",] = swapped
    crossing = []
    steps = {1: NY // 2, -1: NY // 2 - 1}
    for k in range(sections):
        ended = []
        for way in (1, -1):
            for i in range(steps[way]):

                def advance(k=k, i=i, way=way, ended=ended):
                    rs_copy(k, i, way).wait_recv()
                    if i < steps[way] - 1:
                        rs_send(k, i + 1, way)
                    else:
                        ended.append(way)
                    if len(ended) == 2:
                        ended.append(0)
                        ahead = (owner(k)[0] - y + NY) % NY
                        mine_out[k] = jnp.where(
                            ahead == 0, stored(k, y), jnp.where(ahead <= 3, left_in[k, 2], right_in[k, 3]))
                        if not crossing:
                            crossing.append(k)
                            answered(2, greets_h)
                        go(cross_copy(k))

                def gathered(k=k, i=i, way=way):
                    ag_copy(k, i, way).wait_recv()
                    if i < steps[way] - 1:
                        go(ag_copy(k, i + 1, way))
                    go(sib_copy(k, way * (i + 1)))

                events["rs", k, i, way] = advance
                events["ag", k, i, way] = gathered

        def crossed(k=k):
            cross_copy(k).wait_recv()
            panel[k, share_rows(y, c), :] = jnp.where(owner(k)[1] == h, mine_out[k], other_in[k])
            for way in (1, -1):
                go(ag_copy(k, 0, way))
            go(sib_copy(k, 0))

        events["cross", k] = crossed
        last[k].extend(sib_copy(k, d) for d in range(-3, 5))

    go(swap)
    for k in range(sections):
        for way in (1, -1):
            go(z_copy(k, 1, way))
        for way in (1, -1):
            go(x_copy(k, 0, way))
    for copy in labels:
        copy.wait()
    for k in range(sections):
        find_slots(k, occ_ref, pair_ref, row * (out_ref.shape[0] // TILE), index_ref, count_ref)
    for key in ORDER:
        events.pop(key)()
    assert not events
    for k in range(sections):
        if k == sections - 1:
            for copy in sent:
                copy.wait_send()
        for copy in last[k]:
            copy.wait_recv()
        multiply(k, index_ref, count_ref, panel, held[k], out_ref)


def on_device(amplitudes, integrals, owner_column, occ_irrep, pair_irrep):
    tiles_here, slots, tile = amplitudes.shape[1:4]
    sections, _, columns = integrals.shape
    rows = tiles_here * slots * tile
    half, share = rows // NC, rows // NC // NY
    f32 = jnp.float32
    dma = pltpu.SemaphoreType.DMA
    smem = functools.partial(pltpu.SMEM, dtype=jnp.int32)
    return pl.pallas_call(
        kernel,
        out_shape=jax.ShapeDtypeStruct((tiles_here * tile, columns), f32),
        in_specs=[pl.BlockSpec(memory_space=pl.ANY)] * 5,
        out_specs=pl.BlockSpec(memory_space=pltpu.VMEM),
        scratch_shapes=[
            smem(owner_column.shape),
            smem(occ_irrep.shape),
            smem(pair_irrep.shape),
            smem((sections * tiles_here * slots,)),
            smem((sections * tiles_here,)),
            pltpu.VMEM((NX, NZ, tile, columns), f32),
            pltpu.VMEM((NX, NZ, tile, columns), f32),
            pltpu.VMEM((sections, rows, tile), f32),
            pltpu.VMEM((NC, half, tile), f32),
            pltpu.VMEM((sections, 4, share, tile), f32),
            pltpu.VMEM((sections, 4, share, tile), f32),
            pltpu.VMEM((sections, 3, share, tile), f32),
            pltpu.VMEM((sections, 3, share, tile), f32),
            pltpu.VMEM((sections, share, tile), f32),
            pltpu.VMEM((sections, share, tile), f32),
            dma((4 + sections,)),
            dma((2, sections, 3, 2)),
            dma((2, sections, 4, 4)),
            dma((2, sections, 4)),
            dma((2, sections, 3, 2)),
            dma((2, sections, 4, 2)),
            dma((2, sections, 4, 2)),
            dma((2, sections + 1, 8)),
            dma((2, sections)),
            pltpu.SemaphoreType.REGULAR((3,)),
        ],
        compiler_params=pltpu.CompilerParams(
            collective_id=0, has_side_effects=True, vmem_limit_bytes=48 * 1024 * 1024
        ),
        name="ladder",
    )(*(pltpu.with_memory_space_constraint(v, pltpu.HBM)
        for v in (owner_column, occ_irrep, pair_irrep, amplitudes.reshape(rows, tile), integrals)))


def solution(mesh):
    return jax.shard_map(
        on_device,
        mesh=mesh,
        in_specs=(P("col", "row", None, None, None), P(None, "row", "col"), P(), P(), P()),
        out_specs=P("row", "col"),
        check_vma=False,
    )
```

```python
import functools

import jax
import jax.numpy as jnp
from jax import lax
from jax.experimental import pallas as pl
from jax.experimental.pallas import tpu as pltpu
from jax.sharding import PartitionSpec as P

MESH = pl.DeviceIdType.MESH
NX, NZ, NY, NH, NC = 4, 4, 8, 2, 2
TILE = 128
X_ROWS = (24, 24)
STREAMS = 2
OFFSETS = (0, -1, 1, -2, 2, -3, 3)
ORDER = (
    ('swap',), ('fs', 0), ('fs', 1), ('z', 0, 1, 1), ('x', 0, 0, 1), ('z', 0, 1, -1), ('rs', 0, 0, 1),
    ('rs', 1, 0, 1), ('rs', 0, 0, -1), ('f', 0, -1), ('z', 1, 1, -1), ('z', 1, 1, 1), ('rs', 0, 1, 1),
    ('rs', 1, 0, -1), ('f', 1, -1), ('f', 0, 1), ('rs', 1, 1, 1), ('f', 1, 1), ('z', 0, 2, 1), ('z', 0, 2, -1),
    ('rs', 0, 1, -1), ('rs', 0, 2, 1), ('rs', 0, 2, -1), ('rs', 1, 1, -1), ('rs', 1, 2, 1), ('rs', 0, 3, 1),
    ('x', 0, 0, -1), ('rs', 1, 2, -1), ('rs', 1, 3, 1), ('z', 0, 3, 1), ('x', 0, -1, -1), ('z', 1, 2, 1),
    ('z', 1, 2, -1), ('x', 0, -3, -1), ('z', 0, 3, -1), ('x', 0, 1, -1), ('x', 0, -1, 1), ('x', 1, 0, 1), ('fz', 0),
    ('cross', 0), ('x', 0, 2, -1), ('x', 0, 1, 1), ('cross', 1), ('x', 0, 3, 1), ('fz', 1), ('ag', 0, 0, -1),
    ('ag', 0, 0, 1), ('x', 0, -2, 1), ('z', 1, 3, -1), ('x', 1, 0, -1), ('z', 1, 3, 1), ('c', 0, 1, 1),
    ('x', 0, 2, 1), ('x', 0, 3, -1), ('c', 0, 1, -1), ('ag', 1, 0, 1), ('ag', 1, 0, -1), ('x', 1, 1, 1),
    ('x', 1, 2, 1), ('ag', 0, 1, 1), ('x', 0, -2, -1), ('x', 1, -2, -1), ('c', 1, 1, -1), ('c', 1, 1, 1),
    ('x', 0, -3, 1), ('x', 1, 1, -1), ('ag', 1, 1, 1), ('x', 1, -1, -1), ('ag', 1, 1, -1), ('ag', 0, 1, -1),
    ('x', 1, -1, 1), ('c', 0, 2, 1), ('c', 0, 2, -1), ('ag', 0, 2, 1), ('x', 1, -3, -1), ('x', 1, 3, -1),
    ('x', 1, -2, 1), ('ag', 1, 2, 1), ('x', 1, 3, 1), ('c', 1, 2, 1), ('c', 1, 2, -1), ('x', 1, 2, -1),
    ('ag', 1, 2, -1), ('x', 1, -3, 1), ('ag', 0, 3, 1), ('ag', 0, 2, -1), ('ag', 1, 3, 1),
)


class Copy:
    def __init__(self, src, dst, landing, send, recv, device, sends=None, receives=None):
        self.out = (src, dst, send, recv, device)
        self.into = (landing, landing, send, recv, device)
        self.sends, self.receives = sends, receives

    def start(self):
        guarded(self.sends, lambda: remote(*self.out).start())

    def wait_recv(self):
        guarded(self.receives, lambda: remote(*self.into).wait_recv())

    def wait_send(self):
        guarded(self.sends, lambda: remote(*self.out).wait_send())


def remote(src, dst, send, recv, device):
    return pltpu.make_async_remote_copy(
        src_ref=src, dst_ref=dst, send_sem=send, recv_sem=recv, device_id=device, device_id_type=MESH
    )


def guarded(condition, action):
    if condition is None:
        action()
    else:
        pl.when(condition)(action)


def find_slots(k, occ_ref, pair_ref, first, index_ref, count_ref):
    positions, tiles = pair_ref.shape[1], count_ref.shape[0] // pair_ref.shape[0]
    slots = index_ref.shape[0] // count_ref.shape[0]

    def one(o, carry):
        label = occ_ref[first + o]
        count = jnp.int32(0)
        index = [jnp.int32(0)] * slots
        for t in range(positions):
            match = pair_ref[k, t] == label
            for s in range(min(slots, t + 1)):
                index[s] = jnp.where(match & (count == s), t, index[s])
            count = count + match.astype(jnp.int32)
        for s in range(slots):
            index_ref[(k * tiles + o) * slots + s] = index[s]
        count_ref[k * tiles + o] = count
        return carry

    lax.fori_loop(0, tiles, one, 0)


def multiply(k, index_ref, count_ref, panel, held, out_ref):
    tiles = out_ref.shape[0] // TILE
    slots = panel.shape[1] // out_ref.shape[0]
    bf, f32 = jnp.bfloat16, jnp.float32
    dot = functools.partial(jnp.dot, preferred_element_type=f32)

    def split(value):
        high = value.astype(bf)
        return high, (value - high.astype(f32)).astype(bf)

    def one(o, carry):
        here = pl.ds(pl.multiple_of(o * TILE, TILE), TILE)
        count = count_ref[k * tiles + o]
        total = None if k == 0 else out_ref[here, :]
        for pair in range(slots // 2):
            left, right = [], []
            for s in (2 * pair, 2 * pair + 1):
                rows = pl.multiple_of((o * slots + s) * TILE, TILE)
                tile = panel[k, pl.ds(rows, TILE), :]
                left.append(jnp.where(count > s, tile, 0.0))
                t = index_ref[(k * tiles + o) * slots + s]
                right.append(held[t // NZ, t % NZ])
            a_high, a_low = split(jnp.concatenate(left, axis=1))
            b_high, b_low = split(jnp.concatenate(right, axis=0))
            both = dot(jnp.concatenate([a_high, a_low], axis=0), b_high)
            part = both[:TILE] + (both[TILE:] + dot(a_high, b_low))
            total = part if total is None else total + part
        out_ref[here, :] = total
        return carry

    lax.fori_loop(0, tiles, one, 0, unroll=True)


def kernel(owner_hbm, occ_hbm, pair_hbm, amp_ref, int_ref, out_ref, owner_ref, occ_ref, pair_ref, index_ref, count_ref,
           held_0, held_1, panel, both, right_out, right_in,
           left_out, left_in, mine_out, other_in, local_sem, z_sem, x_sem, xf_sem, xz_sem, rs_sem, ag_sem, sib_sem,
           cross_sem, swap_sem, ready_sem):
    row, col = lax.axis_index("row"), lax.axis_index("col")
    x, z = row // NZ, row % NZ
    y, h, c = col // (NH * NC), (col // NC) % NH, col % NC

    def device(dx=0, dz=0, dy=0, flip_h=False, flip_c=False):
        h2 = 1 - h if flip_h else h
        c2 = 1 - c if flip_c else c
        return (((x + dx + NX) % NX) * NZ + z + dz, ((y + dy + NY) % NY) * (NH * NC) + h2 * NC + c2)

    held = (held_0, held_1)
    sections = int_ref.shape[0]
    half = amp_ref.shape[0] // NC
    share = half // NY
    events, last, sent = {}, [[] for _ in range(sections)], []

    def go(copy):
        copy.start()
        sent.append(copy)

    barrier = pltpu.get_barrier_semaphore()
    greets_up, greets_down, greets_h = y < NY // 2, (y == 0) | (y > NY // 2), h == 0
    waits_up, waits_down, waits_h = y >= NY // 2, (y > 0) & (y <= NY // 2), h == 1

    def greet(partner, condition=None):
        guarded(condition, lambda: pl.semaphore_signal(barrier, inc=1, device_id=partner, device_id_type=MESH))

    greet(device(dx=1))
    greet(device(dx=-1))
    greet(device(flip_c=True))
    greet(device(dz=-1), z > 0)
    greet(device(dz=1), z < NZ - 1)
    greet(device(dy=1), greets_up)
    greet(device(dy=-1), greets_down)
    greet(device(flip_h=True), greets_h)
    peers = jnp.int32(3)
    for condition in (z > 0, z < NZ - 1, waits_up, waits_down, waits_h):
        peers = peers + condition.astype(jnp.int32)

    def answer(n, partner, condition):
        guarded(condition, lambda: pl.semaphore_signal(
            ready_sem.at[n], inc=1, device_id=partner, device_id_type=MESH))

    def answered(n, condition):
        guarded(condition, lambda: pl.semaphore_wait(ready_sem.at[n], 1))

    own_ints = [pltpu.make_async_copy(int_ref.at[k], held[k].at[x, z], local_sem.at[1 + k]) for k in range(sections)]
    labels = [
        pltpu.make_async_copy(src, dst, local_sem.at[1 + sections + n])
        for n, (src, dst) in enumerate(((owner_hbm, owner_ref), (occ_hbm, occ_ref), (pair_hbm, pair_ref)))
    ]
    own_half = pltpu.make_async_copy(
        amp_ref.at[pl.ds(pl.multiple_of(c * half, 8), half), :], both.at[c], local_sem.at[0])
    for copy in (*labels, *own_ints):
        copy.start()
    own_half.start()
    pl.semaphore_wait(barrier, peers)
    answer(1, device(dy=1), waits_up)
    answer(0, device(dy=-1), waits_down)
    answer(2, device(flip_h=True), waits_h)

    mid = [((TILE - first) // 8 + k) // 2 * 8 for k, first in enumerate(X_ROWS)]
    zr = [pl.ds(first, TILE - first) for first in X_ROWS]
    low = [pl.ds(first, m) for first, m in zip(X_ROWS, mid)]
    high = [pl.ds(first + m, TILE - first - m) for first, m in zip(X_ROWS, mid)]

    def z_copy(k, s, way):
        src = int_ref.at[k, zr[k]] if s == 1 else held[k].at[x, z - way * (s - 1), zr[k]]
        to = held[k].at[x, z - way * (s - 1), zr[k]]
        frm = held[k].at[x, z - way * s, zr[k]]
        if way > 0:
            sends, receives = (z < NZ - 1) & (z - (s - 1) >= 0), z - s >= 0
        else:
            sends, receives = (z > 0) & (z + (s - 1) <= NZ - 1), z + s <= NZ - 1
        w = 0 if way > 0 else 1
        return Copy(src, to, frm, z_sem.at[0, k, s - 1, w], z_sem.at[1, k, s - 1, w], device(dz=way), sends, receives)

    def x_copy(k, d, way):
        zz = z + d
        valid = None if d == 0 else (zz >= 0) & (zz <= NZ - 1)
        src = int_ref.at[k, zr[k]] if d == 0 else held[k].at[x, zz, zr[k]]
        w = 0 if way > 0 else 1
        return Copy(src, held[k].at[x, zz, zr[k]], held[k].at[(x - way + NX) % NX, zz, zr[k]],
                    x_sem.at[0, k, zz, w], x_sem.at[1, k, zz, w], device(dx=way), valid, valid)

    def x_forward(k, d, way):
        zz = z + d
        valid = None if d == 0 else (zz >= 0) & (zz <= NZ - 1)
        rows = low[k] if way > 0 else high[k]
        xs = (x - way + NX) % NX
        w = 2 if way > 0 else 3
        return Copy(held[k].at[xs, zz, rows], held[k].at[xs, zz, rows], held[k].at[(x + 2) % NX, zz, rows],
                    x_sem.at[0, k, zz, w], x_sem.at[1, k, zz, w], device(dx=way), valid, valid)

    for k in range(sections):
        for d in OFFSETS:
            if d:
                way, s = (1, -d) if d < 0 else (-1, d)

                def arrived(k=k, d=d, way=way, s=s):
                    z_copy(k, s, way).wait_recv()
                    if s < NZ - 1:
                        go(z_copy(k, s + 1, way))
                    for side in (1, -1):
                        go(x_copy(k, d, side))

                events["z", k, s, way] = arrived
            for way in (1, -1):

                def passed(k=k, d=d, way=way):
                    x_copy(k, d, way).wait_recv()
                    go(x_forward(k, d, way))

                events["x", k, d, way] = passed
                last[k].append(x_forward(k, d, way))

    cut = [(first // 8 + k) // 2 * 8 for k, first in enumerate(X_ROWS)]
    xr = [pl.ds(0, first) for first in X_ROWS]
    xlow = [pl.ds(0, m) for m in cut]
    xhigh = [pl.ds(m, first - m) for first, m in zip(X_ROWS, cut)]

    def f_copy(k, way):
        w = 0 if way > 0 else 1
        return Copy(int_ref.at[k, xr[k]], held[k].at[x, z, xr[k]], held[k].at[(x - way + NX) % NX, z, xr[k]],
                    xf_sem.at[0, k, w], xf_sem.at[1, k, w], device(dx=way))

    def f_forward(k, way):
        rows = xlow[k] if way > 0 else xhigh[k]
        xs = (x - way + NX) % NX
        w = 2 if way > 0 else 3
        return Copy(held[k].at[xs, z, rows], held[k].at[xs, z, rows], held[k].at[(x + 2) % NX, z, rows],
                    xf_sem.at[0, k, w], xf_sem.at[1, k, w], device(dx=way))

    def fz_copy(k, s, way):
        to = held[k].at[:, z - way * (s - 1), xr[k]]
        frm = held[k].at[:, z - way * s, xr[k]]
        if way > 0:
            sends, receives = (z < NZ - 1) & (z - (s - 1) >= 0), z - s >= 0
        else:
            sends, receives = (z > 0) & (z + (s - 1) <= NZ - 1), z + s <= NZ - 1
        w = 0 if way > 0 else 1
        return Copy(to, to, frm, xz_sem.at[0, k, s - 1, w], xz_sem.at[1, k, s - 1, w], device(dz=way), sends, receives)

    for k in range(sections):

        def spread(k=k):
            for way in (1, -1):
                go(f_copy(k, way))

        events["fs", k] = spread
        for way in (1, -1):

            def near(k=k, way=way):
                f_copy(k, way).wait_recv()
                go(f_forward(k, way))

            events["f", k, way] = near
            for s in range(1, NZ - 1):

                def climb(k=k, s=s, way=way):
                    fz_copy(k, s, way).wait_recv()
                    go(fz_copy(k, s + 1, way))

                events["c", k, s, way] = climb
            last[k].append(fz_copy(k, NZ - 1, way))

        def far(k=k):
            own_ints[k].wait()
            for way in (1, -1):
                f_forward(k, way).wait_recv()
            for way in (1, -1):
                go(fz_copy(k, 1, way))

        events["fz", k] = far

    def half_rows(core):
        return pl.ds(pl.multiple_of(core * half, 8), half)

    def swap_copy(n):
        j = (y + NY // 2 + (-(n // 2) if n % 2 == 0 else n // 2 + 1)) % NY

        def rows_of(core):
            return pl.ds(pl.multiple_of(core * half + j * share, 8), share)

        part = pl.ds(pl.multiple_of(j * share, 8), share)
        return Copy(amp_ref.at[rows_of(1 - c), :], both.at[c, part, :], both.at[1 - c, part, :],
                    swap_sem.at[0, n], swap_sem.at[1, n], device(flip_c=True))

    def owner(k):
        col_k = owner_ref[k]
        return col_k // (NH * NC), (col_k // NC) % NH, col_k % NC

    pieces = STREAMS // sections
    piece = share // pieces
    have = set()

    def need(n):
        if n not in have:
            have.add(n)
            swap_copy(n).wait_recv()

    def stored(q, j):
        rows = pl.ds(pl.multiple_of(j * share + q % pieces * piece, 8), piece)
        return jnp.where(owner(q // pieces)[2] == 0, both[0, rows, :], both[1, rows, :])

    def rs_copy(q, i, way):
        w = 0 if way > 0 else 1
        src, dst = (right_out, right_in) if way > 0 else (left_out, left_in)
        return Copy(src.at[q, i], dst.at[q, i], dst.at[q, i], rs_sem.at[0, q, i, w], rs_sem.at[1, q, i, w], device(dy=way))

    def rs_send(q, i, way):
        j = (y + 4 - i) % NY if way > 0 else (y - 3 + i + NY) % NY
        src, dst = (right_out, right_in) if way > 0 else (left_out, left_in)
        need(2 * i + (way < 0))
        value = stored(q, j)
        if i:
            value = jnp.where(owner(q // pieces)[0] == y, value, dst[q, i - 1])
        src[q, i] = value
        go(rs_copy(q, i, way))

    def cross_copy(q):
        return Copy(mine_out.at[q], other_in.at[q], other_in.at[q], cross_sem.at[0, q], cross_sem.at[1, q],
                    device(flip_h=True))

    def share_rows(q, j, core):
        return pl.ds(pl.multiple_of(core * half + j * share + q % pieces * piece, 8), piece)

    def ag_copy(q, i, way):
        j = (y - way * i + NY) % NY
        g = (y - way * (i + 1) + NY) % NY
        w = 0 if way > 0 else 1
        return Copy(panel.at[q // pieces, share_rows(q, j, c), :], panel.at[q // pieces, share_rows(q, j, c), :], panel.at[q // pieces, share_rows(q, g, c), :],
                    ag_sem.at[0, q, i, w], ag_sem.at[1, q, i, w], device(dy=way))

    def sib_copy(q, d):
        j = (y - d + NY) % NY
        n = d + 3
        return Copy(panel.at[q // pieces, share_rows(q, j, c), :], panel.at[q // pieces, share_rows(q, j, c), :], panel.at[q // pieces, share_rows(q, j, 1 - c), :],
                    sib_sem.at[0, q, n], sib_sem.at[1, q, n], device(flip_c=True))

    def swapped():
        own_half.wait()
        answered(0, greets_up)
        answered(1, greets_down)
        for q in range(STREAMS):
            for way in (1, -1):
                rs_send(q, 0, way)

    events["swap",] = swapped
    crossing = []
    steps = {1: NY // 2, -1: NY // 2 - 1}
    for q in range(STREAMS):
        ended = []
        for way in (1, -1):
            for i in range(steps[way]):

                def advance(q=q, i=i, way=way, ended=ended):
                    rs_copy(q, i, way).wait_recv()
                    if i < steps[way] - 1:
                        rs_send(q, i + 1, way)
                    else:
                        ended.append(way)
                    if len(ended) == 2:
                        ended.append(0)
                        need(NY - 1)
                        ahead = (owner(q // pieces)[0] - y + NY) % NY
                        mine_out[q] = jnp.where(
                            ahead == 0, stored(q, y), jnp.where(ahead <= 3, left_in[q, 2], right_in[q, 3]))
                        if not crossing:
                            crossing.append(q)
                            answered(2, greets_h)
                        go(cross_copy(q))

                def gathered(q=q, i=i, way=way):
                    ag_copy(q, i, way).wait_recv()
                    if i < steps[way] - 1:
                        go(ag_copy(q, i + 1, way))
                    go(sib_copy(q, way * (i + 1)))

                events["rs", q, i, way] = advance
                events["ag", q, i, way] = gathered

        def crossed(q=q):
            cross_copy(q).wait_recv()
            panel[q // pieces, share_rows(q, y, c), :] = jnp.where(owner(q // pieces)[1] == h, mine_out[q], other_in[q])
            for way in (1, -1):
                go(ag_copy(q, 0, way))
            go(sib_copy(q, 0))

        events["cross", q] = crossed
        last[q // pieces].extend(sib_copy(q, d) for d in range(-3, 5))

    for n in range(NY):
        go(swap_copy(n))
    for k in range(sections):
        for way in (1, -1):
            go(z_copy(k, 1, way))
        for way in (1, -1):
            go(x_copy(k, 0, way))
    for copy in labels:
        copy.wait()
    for k in range(sections):
        find_slots(k, occ_ref, pair_ref, row * (out_ref.shape[0] // TILE), index_ref, count_ref)
    for key in ORDER:
        events.pop(key)()
    assert not events
    for k in range(sections):
        if k == sections - 1:
            for copy in sent:
                copy.wait_send()
        for copy in last[k]:
            copy.wait_recv()
        multiply(k, index_ref, count_ref, panel, held[k], out_ref)


def on_device(amplitudes, integrals, owner_column, occ_irrep, pair_irrep):
    tiles_here, slots, tile = amplitudes.shape[1:4]
    sections, _, columns = integrals.shape
    rows = tiles_here * slots * tile
    half, share = rows // NC, rows // NC // NY
    piece = share * sections // STREAMS
    f32 = jnp.float32
    dma = pltpu.SemaphoreType.DMA
    smem = functools.partial(pltpu.SMEM, dtype=jnp.int32)
    return pl.pallas_call(
        kernel,
        out_shape=jax.ShapeDtypeStruct((tiles_here * tile, columns), f32),
        in_specs=[pl.BlockSpec(memory_space=pl.ANY)] * 5,
        out_specs=pl.BlockSpec(memory_space=pltpu.VMEM),
        scratch_shapes=[
            smem(owner_column.shape),
            smem(occ_irrep.shape),
            smem(pair_irrep.shape),
            smem((sections * tiles_here * slots,)),
            smem((sections * tiles_here,)),
            pltpu.VMEM((NX, NZ, tile, columns), f32),
            pltpu.VMEM((NX, NZ, tile, columns), f32),
            pltpu.VMEM((sections, rows, tile), f32),
            pltpu.VMEM((NC, half, tile), f32),
            pltpu.VMEM((STREAMS, 4, piece, tile), f32),
            pltpu.VMEM((STREAMS, 4, piece, tile), f32),
            pltpu.VMEM((STREAMS, 3, piece, tile), f32),
            pltpu.VMEM((STREAMS, 3, piece, tile), f32),
            pltpu.VMEM((STREAMS, piece, tile), f32),
            pltpu.VMEM((STREAMS, piece, tile), f32),
            dma((4 + sections,)),
            dma((2, sections, 3, 2)),
            dma((2, sections, 4, 4)),
            dma((2, sections, 4)),
            dma((2, sections, 3, 2)),
            dma((2, STREAMS, 4, 2)),
            dma((2, STREAMS, 4, 2)),
            dma((2, STREAMS, 8)),
            dma((2, STREAMS)),
            dma((2, NY)),
            pltpu.SemaphoreType.REGULAR((3,)),
        ],
        compiler_params=pltpu.CompilerParams(
            collective_id=0, has_side_effects=True, vmem_limit_bytes=48 * 1024 * 1024
        ),
        name="ladder",
    )(*(pltpu.with_memory_space_constraint(v, pltpu.HBM)
        for v in (owner_column, occ_irrep, pair_irrep, amplitudes.reshape(rows, tile), integrals)))


def solution(mesh):
    return jax.shard_map(
        on_device,
        mesh=mesh,
        in_specs=(P("col", "row", None, None, None), P(None, "row", "col"), P(), P(), P()),
        out_specs=P("row", "col"),
        check_vma=False,
    )
```

```python
import functools

import jax
import jax.numpy as jnp
from jax import lax
from jax.experimental import pallas as pl
from jax.experimental.pallas import tpu as pltpu
from jax.sharding import PartitionSpec as P

MESH = pl.DeviceIdType.MESH
NX, NZ, NY, NH, NC = 4, 4, 8, 2, 2
TILE = 128
X_ROWS = (24, 24)
STREAMS = 2
OFFSETS = (0, -1, 1, -2, 2, -3, 3)
ORDER = (
    ('fs', 0), ('fs', 1), ('swap',), ('z', 0, 1, 1), ('x', 0, 0, 1), ('z', 0, 1, -1), ('rs', 0, 0, 1),
    ('rs', 1, 0, 1), ('rs', 0, 0, -1), ('f', 0, -1), ('z', 1, 1, -1), ('z', 1, 1, 1), ('rs', 0, 1, 1),
    ('rs', 1, 0, -1), ('f', 1, -1), ('f', 0, 1), ('rs', 1, 1, 1), ('f', 1, 1), ('z', 0, 2, 1), ('z', 0, 2, -1),
    ('rs', 0, 1, -1), ('rs', 0, 2, 1), ('rs', 0, 2, -1), ('rs', 1, 1, -1), ('rs', 1, 2, 1), ('rs', 0, 3, 1),
    ('x', 0, 0, -1), ('rs', 1, 2, -1), ('rs', 1, 3, 1), ('z', 0, 3, 1), ('x', 0, -1, -1), ('z', 1, 2, 1),
    ('z', 1, 2, -1), ('x', 0, -3, -1), ('z', 0, 3, -1), ('x', 0, 1, -1), ('x', 0, -1, 1), ('x', 1, 0, 1), ('fz', 0),
    ('cross', 0), ('x', 0, 2, -1), ('x', 0, 1, 1), ('cross', 1), ('x', 0, 3, 1), ('fz', 1), ('ag', 0, 0, -1),
    ('ag', 0, 0, 1), ('x', 0, -2, 1), ('z', 1, 3, -1), ('x', 1, 0, -1), ('z', 1, 3, 1), ('c', 0, 1, 1),
    ('x', 0, 2, 1), ('x', 0, 3, -1), ('c', 0, 1, -1), ('ag', 1, 0, 1), ('ag', 1, 0, -1), ('x', 1, 1, 1),
    ('x', 1, 2, 1), ('ag', 0, 1, 1), ('x', 0, -2, -1), ('x', 1, -2, -1), ('c', 1, 1, -1), ('c', 1, 1, 1),
    ('x', 0, -3, 1), ('x', 1, 1, -1), ('ag', 1, 1, 1), ('x', 1, -1, -1), ('ag', 1, 1, -1), ('ag', 0, 1, -1),
    ('x', 1, -1, 1), ('c', 0, 2, 1), ('c', 0, 2, -1), ('ag', 0, 2, 1), ('x', 1, -3, -1), ('x', 1, 3, -1),
    ('x', 1, -2, 1), ('ag', 1, 2, 1), ('x', 1, 3, 1), ('c', 1, 2, 1), ('c', 1, 2, -1), ('x', 1, 2, -1),
    ('ag', 1, 2, -1), ('x', 1, -3, 1), ('ag', 0, 3, 1), ('ag', 0, 2, -1), ('ag', 1, 3, 1),
)


class Copy:
    def __init__(self, src, dst, landing, send, recv, device, sends=None, receives=None):
        self.out = (src, dst, send, recv, device)
        self.into = (landing, landing, send, recv, device)
        self.sends, self.receives = sends, receives

    def start(self):
        guarded(self.sends, lambda: remote(*self.out).start())

    def wait_recv(self):
        guarded(self.receives, lambda: remote(*self.into).wait_recv())

    def wait_send(self):
        guarded(self.sends, lambda: remote(*self.out).wait_send())


def remote(src, dst, send, recv, device):
    return pltpu.make_async_remote_copy(
        src_ref=src, dst_ref=dst, send_sem=send, recv_sem=recv, device_id=device, device_id_type=MESH
    )


def guarded(condition, action):
    if condition is None:
        action()
    else:
        pl.when(condition)(action)


def find_slots(k, occ_ref, pair_ref, first, index_ref, count_ref):
    positions, tiles = pair_ref.shape[1], count_ref.shape[0] // pair_ref.shape[0]
    slots = index_ref.shape[0] // count_ref.shape[0]

    def one(o, carry):
        label = occ_ref[first + o]
        count = jnp.int32(0)
        index = [jnp.int32(0)] * slots
        for t in range(positions):
            match = pair_ref[k, t] == label
            for s in range(min(slots, t + 1)):
                index[s] = jnp.where(match & (count == s), t, index[s])
            count = count + match.astype(jnp.int32)
        for s in range(slots):
            index_ref[(k * tiles + o) * slots + s] = index[s]
        count_ref[k * tiles + o] = count
        return carry

    lax.fori_loop(0, tiles, one, 0)


def multiply(k, index_ref, count_ref, panel, held, out_ref):
    tiles = out_ref.shape[0] // TILE
    slots = panel.shape[1] // out_ref.shape[0]
    bf, f32 = jnp.bfloat16, jnp.float32
    dot = functools.partial(jnp.dot, preferred_element_type=f32)

    def split(value):
        high = value.astype(bf)
        return high, (value - high.astype(f32)).astype(bf)

    def one(o, carry):
        here = pl.ds(pl.multiple_of(o * TILE, TILE), TILE)
        count = count_ref[k * tiles + o]
        total = None if k == 0 else out_ref[here, :]
        for pair in range(slots // 2):
            left, right = [], []
            for s in (2 * pair, 2 * pair + 1):
                rows = pl.multiple_of((o * slots + s) * TILE, TILE)
                tile = panel[k, pl.ds(rows, TILE), :]
                left.append(jnp.where(count > s, tile, 0.0))
                t = index_ref[(k * tiles + o) * slots + s]
                right.append(held[t // NZ, t % NZ])
            a_high, a_low = split(jnp.concatenate(left, axis=1))
            b_high, b_low = split(jnp.concatenate(right, axis=0))
            both = dot(jnp.concatenate([a_high, a_low], axis=0), b_high)
            part = both[:TILE] + (both[TILE:] + dot(a_high, b_low))
            total = part if total is None else total + part
        out_ref[here, :] = total
        return carry

    lax.fori_loop(0, tiles, one, 0, unroll=True)


def kernel(owner_hbm, occ_hbm, pair_hbm, amp_ref, int_ref, out_ref, owner_ref, occ_ref, pair_ref, index_ref, count_ref,
           held_0, held_1, panel, both, right_out, right_in,
           left_out, left_in, mine_out, other_in, local_sem, z_sem, x_sem, xf_sem, xz_sem, rs_sem, ag_sem, sib_sem,
           cross_sem, swap_sem, ready_sem):
    row, col = lax.axis_index("row"), lax.axis_index("col")
    x, z = row // NZ, row % NZ
    y, h, c = col // (NH * NC), (col // NC) % NH, col % NC

    def device(dx=0, dz=0, dy=0, flip_h=False, flip_c=False):
        h2 = 1 - h if flip_h else h
        c2 = 1 - c if flip_c else c
        return (((x + dx + NX) % NX) * NZ + z + dz, ((y + dy + NY) % NY) * (NH * NC) + h2 * NC + c2)

    held = (held_0, held_1)
    sections = int_ref.shape[0]
    half = amp_ref.shape[0] // NC
    share = half // NY
    events, last, sent = {}, [[] for _ in range(sections)], []

    def go(copy):
        copy.start()
        sent.append(copy)

    barrier = pltpu.get_barrier_semaphore()
    greets_up, greets_down, greets_h = y < NY // 2, (y == 0) | (y > NY // 2), h == 0
    waits_up, waits_down, waits_h = y >= NY // 2, (y > 0) & (y <= NY // 2), h == 1

    def greet(partner, condition=None):
        guarded(condition, lambda: pl.semaphore_signal(barrier, inc=1, device_id=partner, device_id_type=MESH))

    greet(device(dx=1))
    greet(device(dx=-1))
    greet(device(flip_c=True))
    greet(device(dz=-1), z > 0)
    greet(device(dz=1), z < NZ - 1)
    greet(device(dy=1), greets_up)
    greet(device(dy=-1), greets_down)
    greet(device(flip_h=True), greets_h)
    peers = jnp.int32(3)
    for condition in (z > 0, z < NZ - 1, waits_up, waits_down, waits_h):
        peers = peers + condition.astype(jnp.int32)

    def answer(n, partner, condition):
        guarded(condition, lambda: pl.semaphore_signal(
            ready_sem.at[n], inc=1, device_id=partner, device_id_type=MESH))

    def answered(n, condition):
        guarded(condition, lambda: pl.semaphore_wait(ready_sem.at[n], 1))

    own_ints = [pltpu.make_async_copy(int_ref.at[k], held[k].at[x, z], local_sem.at[1 + k]) for k in range(sections)]
    labels = [
        pltpu.make_async_copy(src, dst, local_sem.at[1 + sections + n])
        for n, (src, dst) in enumerate(((owner_hbm, owner_ref), (occ_hbm, occ_ref), (pair_hbm, pair_ref)))
    ]
    own_half = pltpu.make_async_copy(
        amp_ref.at[pl.ds(pl.multiple_of(c * half, 8), half), :], both.at[c], local_sem.at[0])
    for copy in (*labels, *own_ints):
        copy.start()
    own_half.start()
    pl.semaphore_wait(barrier, peers)
    answer(1, device(dy=1), waits_up)
    answer(0, device(dy=-1), waits_down)
    answer(2, device(flip_h=True), waits_h)

    mid = [((TILE - first) // 8 + k) // 2 * 8 for k, first in enumerate(X_ROWS)]
    zr = [pl.ds(first, TILE - first) for first in X_ROWS]
    low = [pl.ds(first, m) for first, m in zip(X_ROWS, mid)]
    high = [pl.ds(first + m, TILE - first - m) for first, m in zip(X_ROWS, mid)]

    def z_copy(k, s, way):
        src = int_ref.at[k, zr[k]] if s == 1 else held[k].at[x, z - way * (s - 1), zr[k]]
        to = held[k].at[x, z - way * (s - 1), zr[k]]
        frm = held[k].at[x, z - way * s, zr[k]]
        if way > 0:
            sends, receives = (z < NZ - 1) & (z - (s - 1) >= 0), z - s >= 0
        else:
            sends, receives = (z > 0) & (z + (s - 1) <= NZ - 1), z + s <= NZ - 1
        w = 0 if way > 0 else 1
        return Copy(src, to, frm, z_sem.at[0, k, s - 1, w], z_sem.at[1, k, s - 1, w], device(dz=way), sends, receives)

    def x_copy(k, d, way):
        zz = z + d
        valid = None if d == 0 else (zz >= 0) & (zz <= NZ - 1)
        src = int_ref.at[k, zr[k]] if d == 0 else held[k].at[x, zz, zr[k]]
        w = 0 if way > 0 else 1
        return Copy(src, held[k].at[x, zz, zr[k]], held[k].at[(x - way + NX) % NX, zz, zr[k]],
                    x_sem.at[0, k, zz, w], x_sem.at[1, k, zz, w], device(dx=way), valid, valid)

    def x_forward(k, d, way):
        zz = z + d
        valid = None if d == 0 else (zz >= 0) & (zz <= NZ - 1)
        rows = low[k] if way > 0 else high[k]
        xs = (x - way + NX) % NX
        w = 2 if way > 0 else 3
        return Copy(held[k].at[xs, zz, rows], held[k].at[xs, zz, rows], held[k].at[(x + 2) % NX, zz, rows],
                    x_sem.at[0, k, zz, w], x_sem.at[1, k, zz, w], device(dx=way), valid, valid)

    for k in range(sections):
        for d in OFFSETS:
            if d:
                way, s = (1, -d) if d < 0 else (-1, d)

                def arrived(k=k, d=d, way=way, s=s):
                    z_copy(k, s, way).wait_recv()
                    if s < NZ - 1:
                        go(z_copy(k, s + 1, way))
                    for side in (1, -1):
                        go(x_copy(k, d, side))

                events["z", k, s, way] = arrived
            for way in (1, -1):

                def passed(k=k, d=d, way=way):
                    x_copy(k, d, way).wait_recv()
                    go(x_forward(k, d, way))

                events["x", k, d, way] = passed
                last[k].append(x_forward(k, d, way))

    cut = [(first // 8 + k) // 2 * 8 for k, first in enumerate(X_ROWS)]
    xr = [pl.ds(0, first) for first in X_ROWS]
    xlow = [pl.ds(0, m) for m in cut]
    xhigh = [pl.ds(m, first - m) for first, m in zip(X_ROWS, cut)]

    def f_copy(k, way):
        w = 0 if way > 0 else 1
        return Copy(int_ref.at[k, xr[k]], held[k].at[x, z, xr[k]], held[k].at[(x - way + NX) % NX, z, xr[k]],
                    xf_sem.at[0, k, w], xf_sem.at[1, k, w], device(dx=way))

    def f_forward(k, way):
        rows = xlow[k] if way > 0 else xhigh[k]
        xs = (x - way + NX) % NX
        w = 2 if way > 0 else 3
        return Copy(held[k].at[xs, z, rows], held[k].at[xs, z, rows], held[k].at[(x + 2) % NX, z, rows],
                    xf_sem.at[0, k, w], xf_sem.at[1, k, w], device(dx=way))

    def fz_copy(k, s, way):
        to = held[k].at[:, z - way * (s - 1), xr[k]]
        frm = held[k].at[:, z - way * s, xr[k]]
        if way > 0:
            sends, receives = (z < NZ - 1) & (z - (s - 1) >= 0), z - s >= 0
        else:
            sends, receives = (z > 0) & (z + (s - 1) <= NZ - 1), z + s <= NZ - 1
        w = 0 if way > 0 else 1
        return Copy(to, to, frm, xz_sem.at[0, k, s - 1, w], xz_sem.at[1, k, s - 1, w], device(dz=way), sends, receives)

    for k in range(sections):

        def spread(k=k):
            for way in (1, -1):
                go(f_copy(k, way))

        events["fs", k] = spread
        for way in (1, -1):

            def near(k=k, way=way):
                f_copy(k, way).wait_recv()
                go(f_forward(k, way))

            events["f", k, way] = near
            for s in range(1, NZ - 1):

                def climb(k=k, s=s, way=way):
                    fz_copy(k, s, way).wait_recv()
                    go(fz_copy(k, s + 1, way))

                events["c", k, s, way] = climb
            last[k].append(fz_copy(k, NZ - 1, way))

        def far(k=k):
            own_ints[k].wait()
            for way in (1, -1):
                f_forward(k, way).wait_recv()
            for way in (1, -1):
                go(fz_copy(k, 1, way))

        events["fz", k] = far

    def swap_copy(n):
        j = (y + NY // 2 + (-(n // 2) if n % 2 == 0 else n // 2 + 1)) % NY

        def rows_of(core):
            return pl.ds(pl.multiple_of(core * half + j * share, 8), share)

        part = pl.ds(pl.multiple_of(j * share, 8), share)
        return Copy(amp_ref.at[rows_of(1 - c), :], both.at[c, part, :], both.at[1 - c, part, :],
                    swap_sem.at[0, n], swap_sem.at[1, n], device(flip_c=True))

    def owner(k):
        col_k = owner_ref[k]
        return col_k // (NH * NC), (col_k // NC) % NH, col_k % NC

    pieces = STREAMS // sections
    piece = share // pieces
    have = set()

    def need(n):
        if n not in have:
            have.add(n)
            swap_copy(n).wait_recv()

    def stored(q, j):
        rows = pl.ds(pl.multiple_of(j * share + q % pieces * piece, 8), piece)
        return jnp.where(owner(q // pieces)[2] == 0, both[0, rows, :], both[1, rows, :])

    def rs_copy(q, i, way):
        w = 0 if way > 0 else 1
        src, dst = (right_out, right_in) if way > 0 else (left_out, left_in)
        return Copy(src.at[q, i], dst.at[q, i], dst.at[q, i], rs_sem.at[0, q, i, w], rs_sem.at[1, q, i, w], device(dy=way))

    def rs_send(q, i, way):
        j = (y + 4 - i) % NY if way > 0 else (y - 3 + i + NY) % NY
        src, dst = (right_out, right_in) if way > 0 else (left_out, left_in)
        need(2 * i + (way < 0))
        value = stored(q, j)
        if i:
            value = jnp.where(owner(q // pieces)[0] == y, value, dst[q, i - 1])
        src[q, i] = value
        go(rs_copy(q, i, way))

    def cross_copy(q):
        return Copy(mine_out.at[q], other_in.at[q], other_in.at[q], cross_sem.at[0, q], cross_sem.at[1, q],
                    device(flip_h=True))

    def share_rows(q, j, core):
        return pl.ds(pl.multiple_of(core * half + j * share + q % pieces * piece, 8), piece)

    def ag_copy(q, i, way):
        j = (y - way * i + NY) % NY
        g = (y - way * (i + 1) + NY) % NY
        w = 0 if way > 0 else 1
        return Copy(panel.at[q // pieces, share_rows(q, j, c), :], panel.at[q // pieces, share_rows(q, j, c), :], panel.at[q // pieces, share_rows(q, g, c), :],
                    ag_sem.at[0, q, i, w], ag_sem.at[1, q, i, w], device(dy=way))

    def sib_copy(q, d):
        j = (y - d + NY) % NY
        n = d + 3
        return Copy(panel.at[q // pieces, share_rows(q, j, c), :], panel.at[q // pieces, share_rows(q, j, c), :], panel.at[q // pieces, share_rows(q, j, 1 - c), :],
                    sib_sem.at[0, q, n], sib_sem.at[1, q, n], device(flip_c=True))

    def swapped():
        own_half.wait()
        answered(0, greets_up)
        answered(1, greets_down)
        for q in range(STREAMS):
            for way in (1, -1):
                rs_send(q, 0, way)

    events["swap",] = swapped
    crossing = []
    steps = {1: NY // 2, -1: NY // 2 - 1}
    for q in range(STREAMS):
        ended = []
        for way in (1, -1):
            for i in range(steps[way]):

                def advance(q=q, i=i, way=way, ended=ended):
                    rs_copy(q, i, way).wait_recv()
                    if i < steps[way] - 1:
                        rs_send(q, i + 1, way)
                    else:
                        ended.append(way)
                    if len(ended) == 2:
                        ended.append(0)
                        need(NY - 1)
                        ahead = (owner(q // pieces)[0] - y + NY) % NY
                        mine_out[q] = jnp.where(
                            ahead == 0, stored(q, y), jnp.where(ahead <= 3, left_in[q, 2], right_in[q, 3]))
                        if not crossing:
                            crossing.append(q)
                            answered(2, greets_h)
                        go(cross_copy(q))

                def gathered(q=q, i=i, way=way):
                    ag_copy(q, i, way).wait_recv()
                    if i < steps[way] - 1:
                        go(ag_copy(q, i + 1, way))
                    go(sib_copy(q, way * (i + 1)))

                events["rs", q, i, way] = advance
                events["ag", q, i, way] = gathered

        def crossed(q=q):
            cross_copy(q).wait_recv()
            panel[q // pieces, share_rows(q, y, c), :] = jnp.where(owner(q // pieces)[1] == h, mine_out[q], other_in[q])
            for way in (1, -1):
                go(ag_copy(q, 0, way))
            go(sib_copy(q, 0))

        events["cross", q] = crossed
        last[q // pieces].extend(sib_copy(q, d) for d in range(-3, 5))

    for n in range(NY):
        go(swap_copy(n))
    for k in range(sections):
        for way in (1, -1):
            go(z_copy(k, 1, way))
        for way in (1, -1):
            go(x_copy(k, 0, way))
    for copy in labels:
        copy.wait()
    for k in range(sections):
        find_slots(k, occ_ref, pair_ref, row * (out_ref.shape[0] // TILE), index_ref, count_ref)
    for key in ORDER:
        events.pop(key)()
    assert not events
    for k in range(sections):
        if k == sections - 1:
            for copy in sent:
                copy.wait_send()
        for copy in last[k]:
            copy.wait_recv()
        multiply(k, index_ref, count_ref, panel, held[k], out_ref)


def on_device(amplitudes, integrals, owner_column, occ_irrep, pair_irrep):
    tiles_here, slots, tile = amplitudes.shape[1:4]
    sections, _, columns = integrals.shape
    rows = tiles_here * slots * tile
    half, share = rows // NC, rows // NC // NY
    piece = share * sections // STREAMS
    f32 = jnp.float32
    dma = pltpu.SemaphoreType.DMA
    smem = functools.partial(pltpu.SMEM, dtype=jnp.int32)
    return pl.pallas_call(
        kernel,
        out_shape=jax.ShapeDtypeStruct((tiles_here * tile, columns), f32),
        in_specs=[pl.BlockSpec(memory_space=pl.ANY)] * 5,
        out_specs=pl.BlockSpec(memory_space=pltpu.VMEM),
        scratch_shapes=[
            smem(owner_column.shape),
            smem(occ_irrep.shape),
            smem(pair_irrep.shape),
            smem((sections * tiles_here * slots,)),
            smem((sections * tiles_here,)),
            pltpu.VMEM((NX, NZ, tile, columns), f32),
            pltpu.VMEM((NX, NZ, tile, columns), f32),
            pltpu.VMEM((sections, rows, tile), f32),
            pltpu.VMEM((NC, half, tile), f32),
            pltpu.VMEM((STREAMS, 4, piece, tile), f32),
            pltpu.VMEM((STREAMS, 4, piece, tile), f32),
            pltpu.VMEM((STREAMS, 3, piece, tile), f32),
            pltpu.VMEM((STREAMS, 3, piece, tile), f32),
            pltpu.VMEM((STREAMS, piece, tile), f32),
            pltpu.VMEM((STREAMS, piece, tile), f32),
            dma((4 + sections,)),
            dma((2, sections, 3, 2)),
            dma((2, sections, 4, 4)),
            dma((2, sections, 4)),
            dma((2, sections, 3, 2)),
            dma((2, STREAMS, 4, 2)),
            dma((2, STREAMS, 4, 2)),
            dma((2, STREAMS, 8)),
            dma((2, STREAMS)),
            dma((2, NY)),
            pltpu.SemaphoreType.REGULAR((3,)),
        ],
        compiler_params=pltpu.CompilerParams(
            collective_id=0, has_side_effects=True, vmem_limit_bytes=48 * 1024 * 1024
        ),
        name="ladder",
    )(*(pltpu.with_memory_space_constraint(v, pltpu.HBM)
        for v in (owner_column, occ_irrep, pair_irrep, amplitudes.reshape(rows, tile), integrals)))


def solution(mesh):
    return jax.shard_map(
        on_device,
        mesh=mesh,
        in_specs=(P("col", "row", None, None, None), P(None, "row", "col"), P(), P(), P()),
        out_specs=P("row", "col"),
        check_vma=False,
    )
```
